32 devices in a mesh: gx: 8 (over y, x, core), gy: 4 (over z).
Axes of the slice: x: 2, y: 2, z: 4, core: 2. Of those that a mesh axis runs over, the one named last changes fastest.
Arguments:
- right_side: float32 [2, 128, 512], P(None, 'gx', 'gy'), may hold values from -160 to 160
- conductivity: float32 [128, 512], P('gx', 'gy'), may hold values from 0.2 to 5
- leaf_inverse: float32 [32, 16, 128, 128], P('gx', 'gy'), may hold values from -1 to 4, as said below
- front_basis: float32 [128, 512, 128], P('gx', 'gy'), may hold values from -0.25 to 0.25
- leaf_transfer: float32 [8, 4, 128, 128], P('gx', 'gy'), may hold values from -0.4375 to 0.4375
- node_transfer: float32 [8, 4, 4, 128, 128], P('gx', 'gy'), may hold values from -1 to 1, as said below
- leaf_front: float32 [8, 4, 128, 128], P('gx', 'gy'), may hold values from -1 to 1, as said below
- node_front: float32 [8, 4, 5, 128, 128], P('gx', 'gy'), may hold values from -1 to 1, as said below
Outputs:
- solution: float32 [2, 128, 512], P(None, 'gx', 'gy')
- residual: float32 [2, 128, 512], P(None, 'gx', 'gy')
- direction: float32 [2, 128, 512], P(None, 'gx', 'gy')
The draws below stay inside these ranges and needn't reach their ends.
Inputs may be any that keep to these rules, and one draw needn't show every extreme that they name: `leaf_inverse`: every block is symmetric and positive definite. `leaf_front`: every matrix is symmetric and positive definite. `node_front`: every matrix is symmetric and positive definite; entry h - 1 is the same for all tiles covered by one node of level h. `node_transfer`: entry h - 1 is the same for all tiles covered by one node of level h.
All inputs are finite; a program needn't handle non-finite values.
Results may differ from the reference program's by a relative error of at most 0.0001.
Values sent between devices are 32-bit elements; how exact they have to be, the bound alone decides.
No kernel may reach another device: no remote copies, remote signals or barrier semaphores. Data moves between devices by JAX's collectives and lax.ppermute only.
A program may use at most 64 MiB of HBM per device.

```python
import math
import jax
import jax.numpy as jnp
from jax import lax

CX = 16
CY = 128
RK = 128
LBX = 4
LBY = 32
RHS = 2
LEAF = 128
TILES_X = 8
TILES_Y = 4
TILES = 32
LEVELS = 5
NX = 128
NY = 512
N_GX = 8
N_GY = 4


def dominant(key, shape, order, off_spread, low_diag, high_diag):
    first_key, second_key = jax.random.split(key)
    uniform_raw = jax.random.uniform(first_key, shape, jnp.float32, -1.0, 1.0)
    symmetric = 0.5 * (uniform_raw + jnp.swapaxes(uniform_raw, -1, -2)) * (off_spread / order)
    diagonal = jax.random.uniform(second_key, shape[:-1], jnp.float32, low_diag, high_diag)
    identity = jnp.eye(order, dtype=jnp.float32)
    return symmetric * (1.0 - identity) + identity * diagonal[..., None]


def draw_right_side(key, part):
    key_list = jax.random.split(jax.random.fold_in(key, 3), 3)
    row_log = jax.random.uniform(key_list[0], (NX,), jnp.float32, 0.0, 1.0)
    col_log = jax.random.uniform(key_list[1], (NY,), jnp.float32, 0.0, 1.0)
    row_place = jnp.arange(NX, dtype=jnp.float32) / max(NX - 1, 1)
    col_place = jnp.arange(NY, dtype=jnp.float32) / max(NY - 1, 1)
    row_scale = jnp.power(10.0, row_log - 0.5) * jnp.power(3.0, row_place - 0.5)
    col_scale = jnp.power(10.0, col_log - 0.5) * jnp.power(3.0, col_place - 0.5)
    scale_grid = row_scale[:, None] * col_scale[None, :]
    rough_part = jnp.clip(jax.random.normal(key_list[2], (RHS, NX, NY), jnp.float32), -5.0, 5.0)
    return rough_part * scale_grid[None, :, :]


def draw_leaf_inverse(key, part):
    return dominant(jax.random.fold_in(key, 5), (NX // LBX, NY // LBY, LEAF, LEAF), LEAF, 1.5, 1.6, 3.2)


def draw_leaf_front(key, part):
    return dominant(jax.random.fold_in(key, 7), (TILES_X, TILES_Y, RK, RK), RK, 0.2, 0.25, 0.5)


def draw_node_transfer(key, part):
    scale = (RK * 7 // 5) ** (-0.5)
    stacked = []
    for height in range(1, LEVELS):
        level_key = jax.random.fold_in(jax.random.fold_in(key, 13), height)
        nodes = jnp.clip(jax.random.normal(level_key, (TILES >> height, RK, RK), jnp.float32), -4.0, 4.0) * scale
        stacked.append(jnp.repeat(nodes, 1 << height, axis=0))
    return jnp.stack(stacked, axis=1).reshape(TILES_X, TILES_Y, LEVELS - 1, RK, RK)


def draw_node_front(key, part):
    stacked = []
    for height in range(1, LEVELS + 1):
        level_key = jax.random.fold_in(jax.random.fold_in(key, 11), height)
        nodes = dominant(level_key, (TILES >> height, RK, RK), RK, 0.2, 0.25, 0.5)
        stacked.append(jnp.repeat(nodes, 1 << height, axis=0))
    return jnp.stack(stacked, axis=1).reshape(TILES_X, TILES_Y, LEVELS, RK, RK)


def shard_levels(key, extent, cuts, least, largest):
    def one(axis_at, blocks):
        draws = jax.random.uniform(jax.random.fold_in(jax.random.fold_in(key, 6), axis_at), (blocks,), jnp.float32, least / len(cuts), largest / len(cuts))
        return jnp.repeat(jnp.exp(draws), extent[axis_at] // blocks).reshape((-1,) + (1,) * (len(extent) - axis_at - 1))

    factor_of = one(*cuts[0])
    for cut in cuts[1:]:
        factor_of = factor_of * one(*cut)
    return factor_of


def bell_draw(stream_key, extent, width, reach, cuts=(), held_as=jnp.bfloat16):
    values = jax.random.normal(stream_key, extent, jnp.float32) * width
    if len(cuts) > 0:
        values = shard_levels(stream_key, extent, cuts, -0.22, 0.18) * values
    return jnp.clip(values, min=-reach, max=reach).astype(held_as)


def setup_inputs(seed: int = 0) -> dict:
    splits = jax.random.split(jax.random.key(seed), 9)
    right_side = draw_right_side(jax.random.fold_in(splits[8], 71), 0)
    conductivity = jnp.clip(jnp.exp(math.log(5.0) - 3.218876 * jax.random.uniform(splits[1], (NX, NY), jnp.float32) ** shard_levels(splits[1], (NX, NY), ((0, 8), (1, 4)), -0.2, 0.2)), 0.2, 5.0)
    leaf_inverse = draw_leaf_inverse(jax.random.fold_in(splits[8], 71), 0)
    front_basis = bell_draw(splits[3], (NX, NY, RK), (CX * CY // 4) ** -0.5, 0.25, ((0, 8), (1, 4)), jnp.float32)
    leaf_transfer = bell_draw(splits[4], (TILES_X, TILES_Y, RK, RK), (RK * 7 // 5) ** -0.5, 0.4375, ((0, 8), (1, 4)), jnp.float32)
    node_transfer = draw_node_transfer(jax.random.fold_in(splits[8], 71), 0)
    leaf_front = draw_leaf_front(jax.random.fold_in(splits[8], 71), 0)
    node_front = draw_node_front(jax.random.fold_in(splits[8], 71), 0)
    return {"right_side": right_side, "conductivity": conductivity, "leaf_inverse": leaf_inverse, "front_basis": front_basis, "leaf_transfer": leaf_transfer, "node_transfer": node_transfer, "leaf_front": leaf_front, "node_front": node_front}


HIGHEST = lax.Precision.HIGHEST


def operate_padded(padded, padded_k):
    extent_x = padded.shape[1] - 2
    extent_y = padded.shape[2] - 2
    center = padded[:, 1:-1, 1:-1]
    center_k = padded_k[1:-1, 1:-1]
    summed = jnp.zeros_like(center)
    for offset_x, offset_y in ((2, 1), (0, 1), (1, 2), (1, 0)):
        beside = padded[:, offset_x:offset_x + extent_x, offset_y:offset_y + extent_y]
        beside_k = padded_k[offset_x:offset_x + extent_x, offset_y:offset_y + extent_y]
        summed = summed + 0.5 * (center_k + beside_k) * (center - beside)
    return summed


def operate(values, conduct):
    padded = jnp.pad(values, ((0, 0), (1, 1), (1, 1)))
    padded_k = jnp.pad(conduct, ((1, 1), (1, 1)))
    return operate_padded(padded, padded_k)


def leaf_apply(values, leaf_inverse):
    count_s, extent_x, extent_y = values.shape
    blocks_x = extent_x // LBX
    blocks_y = extent_y // LBY
    grouped = values.reshape(count_s, blocks_x, LBX, blocks_y, LBY).transpose(0, 1, 3, 2, 4)
    grouped = grouped.reshape(count_s, blocks_x, blocks_y, LBX * LBY)
    mapped = jnp.einsum("xyij,sxyj->sxyi", leaf_inverse, grouped, precision=HIGHEST)
    mapped = mapped.reshape(count_s, blocks_x, blocks_y, LBX, LBY).transpose(0, 1, 3, 2, 4)
    return mapped.reshape(count_s, extent_x, extent_y)


def tree_apply(coeffs, leaf_transfer, node_transfer, leaf_front, node_front):
    devices = coeffs.shape[0]
    levels = devices.bit_length() - 1
    leaf_t = leaf_transfer.reshape(devices, RK, RK)
    node_t = node_transfer.reshape(devices, levels - 1, RK, RK)
    leaf_f = leaf_front.reshape(devices, RK, RK)
    node_f = node_front.reshape(devices, levels, RK, RK)
    uppers = [coeffs]
    moving = jnp.einsum("dsj,djk->dsk", coeffs, leaf_t, precision=HIGHEST)
    uppers.append(moving[0::2] + moving[1::2])
    for height in range(2, levels + 1):
        owners = jnp.arange(devices >> (height - 1), dtype=jnp.int32) * (1 << (height - 1))
        moving = jnp.einsum("dsj,djk->dsk", uppers[height - 1], node_t[owners, height - 2], precision=HIGHEST)
        uppers.append(moving[0::2] + moving[1::2])
    downward = jnp.einsum("dsj,jk->dsk", uppers[levels], node_f[0, levels - 1], precision=HIGHEST)
    for height in range(levels, 1, -1):
        owners = jnp.arange(devices >> (height - 1), dtype=jnp.int32) * (1 << (height - 1))
        parents = jnp.repeat(downward, 2, axis=0)
        downward = jnp.einsum("dsk,djk->dsj", parents, node_t[owners, height - 2], precision=HIGHEST) + jnp.einsum(
            "dsj,djk->dsk", uppers[height - 1], node_f[owners, height - 2], precision=HIGHEST)
    parents = jnp.repeat(downward, 2, axis=0)
    return jnp.einsum("dsk,djk->dsj", parents, leaf_t, precision=HIGHEST) + jnp.einsum(
        "dsj,djk->dsk", coeffs, leaf_f, precision=HIGHEST)


def precondition(values, leaf_inverse, front_basis, leaf_transfer, node_transfer, leaf_front, node_front):
    count_s = values.shape[0]
    near = leaf_apply(values, leaf_inverse)
    tiles = values.reshape(count_s, N_GX, CX, N_GY, CY)
    basis_tiles = front_basis.reshape(N_GX, CX, N_GY, CY, RK)
    coeffs = jnp.einsum("sxayb,xaybk->xysk", tiles, basis_tiles, precision=HIGHEST)
    coeffs = coeffs.reshape(N_GX * N_GY, count_s, RK)
    spread = tree_apply(coeffs, leaf_transfer, node_transfer, leaf_front, node_front)
    spread_t = spread.reshape(N_GX, N_GY, count_s, RK)
    far = jnp.einsum("xysk,xaybk->sxayb", spread_t, basis_tiles, precision=HIGHEST)
    return near + far.reshape(values.shape)


def reference(right_side, conductivity, leaf_inverse, front_basis, leaf_transfer, node_transfer, leaf_front, node_front):
    def apply_inverse(values):
        return precondition(values, leaf_inverse, front_basis, leaf_transfer, node_transfer, leaf_front, node_front)

    first_z = apply_inverse(right_side)
    rz_old = jnp.sum(right_side * first_z, axis=(1, 2))
    applied = operate(first_z, conductivity)
    curvature = jnp.sum(first_z * applied, axis=(1, 2))
    step_size = (rz_old / curvature)[:, None, None]
    solution = step_size * first_z
    residual = right_side - step_size * applied
    second_z = apply_inverse(residual)
    rz_new = jnp.sum(residual * second_z, axis=(1, 2))
    direction = second_z + (rz_new / rz_old)[:, None, None] * first_z
    return (solution, residual, direction)
```

```python
import jax
import jax.numpy as jnp
from jax import lax
from jax.sharding import PartitionSpec as P

LBX = 4
LBY = 32
AXES = ("gx", "gy")
HIGHEST = lax.Precision.HIGHEST


def dot(a, b):
    return jnp.dot(a, b, precision=HIGHEST)


def pair_halo(head, tail, axis):
    count = lax.axis_size(axis)
    odd = lax.rem(lax.axis_index(axis), 2) == 1
    inner = [(i, i ^ 1) for i in range(count)]
    outer = []
    for i in range(1, count - 1, 2):
        outer += [(i, i + 1), (i + 1, i)]
    from_inner = lax.ppermute(jnp.where(odd, head, tail), axis, inner)
    from_outer = lax.ppermute(jnp.where(odd, tail, head), axis, outer)
    return jnp.where(odd, from_inner, from_outer), jnp.where(odd, from_outer, from_inner)


def stencil(values, conductivity):
    stacked = jnp.concatenate([values, conductivity[None]], axis=0)
    up, down = pair_halo(stacked[:, 0, :], stacked[:, -1, :], "gx")
    left, right = pair_halo(stacked[:, :, 0], stacked[:, :, -1], "gy")
    above = jnp.concatenate([up[:, None, :], stacked[:, :-1, :]], axis=1)
    below = jnp.concatenate([stacked[:, 1:, :], down[:, None, :]], axis=1)
    before = jnp.concatenate([left[:, :, None], stacked[:, :, :-1]], axis=2)
    after = jnp.concatenate([stacked[:, :, 1:], right[:, :, None]], axis=2)
    summed = jnp.zeros_like(values)
    for beside in (below, above, after, before):
        summed = summed + 0.5 * (stacked[-1] + beside[-1]) * (values - beside[:-1])
    return summed


def leaf_apply(values, leaf_inverse):
    count_s, extent_x, extent_y = values.shape
    blocks_x = extent_x // LBX
    blocks_y = extent_y // LBY
    grouped = values.reshape(count_s, blocks_x, LBX, blocks_y, LBY).transpose(0, 1, 3, 2, 4)
    grouped = grouped.reshape(count_s, blocks_x, blocks_y, LBX * LBY)
    mapped = jnp.einsum("xyij,sxyj->sxyi", leaf_inverse, grouped, precision=HIGHEST)
    mapped = mapped.reshape(count_s, blocks_x, blocks_y, LBX, LBY).transpose(0, 1, 3, 2, 4)
    return mapped.reshape(count_s, extent_x, extent_y)


def meeting_levels(levels):
    count = 1 << levels
    apart = jnp.arange(count, dtype=jnp.int32) ^ lax.axis_index(AXES).astype(jnp.int32)
    level = sum((apart >= (1 << h)).astype(jnp.int32) for h in range(levels))
    return (level[:, None] == jnp.arange(1, levels + 1)[None, :]).astype(jnp.float32)


def sweep(coeffs, meets, extra, transfers, fronts):
    levels = len(transfers)
    chain = [coeffs]
    for transfer in transfers:
        chain.append(dot(chain[-1], transfer))
    rows = jnp.stack(chain[1:])
    sent = jnp.sum(meets[:, :, None, None] * rows[None], axis=1)
    if extra is not None:
        extra = jnp.broadcast_to(extra[None], (sent.shape[0],) + extra.shape)
        sent = jnp.concatenate([sent, extra], axis=1)
    got = lax.all_to_all(sent, AXES, 0, 0)
    count_s = coeffs.shape[0]
    from_level = jnp.sum(meets[:, :, None, None] * got[:, None, :count_s], axis=0)
    uppers = [coeffs, chain[1] + from_level[0]]
    for height in range(2, levels + 1):
        uppers.append(dot(uppers[-1], transfers[height - 1]) + from_level[height - 1])
    downward = dot(uppers[levels], fronts[levels])
    for height in range(levels, 0, -1):
        downward = dot(downward, transfers[height - 1].T) + dot(uppers[height - 1], fronts[height - 1])
    return downward, (None if extra is None else jnp.sum(got[:, count_s:], axis=0))


def on_device(
    right_side,
    conductivity,
    leaf_inverse,
    front_basis,
    leaf_transfer,
    node_transfer,
    leaf_front,
    node_front,
):
    levels = node_front.shape[2]
    rank = front_basis.shape[-1]
    transfers = [leaf_transfer[0, 0]] + [node_transfer[0, 0, h] for h in range(levels - 1)]
    fronts = [leaf_front[0, 0]] + [node_front[0, 0, h] for h in range(levels)]
    meets = meeting_levels(levels)

    def project(values):
        return jnp.einsum("sab,abk->sk", values, front_basis, precision=HIGHEST)

    def expand(spread):
        return jnp.einsum("sk,abk->sab", spread, front_basis, precision=HIGHEST)

    spread, _ = sweep(project(right_side), meets, None, transfers, fronts)
    first_z = leaf_apply(right_side, leaf_inverse) + expand(spread)
    applied = stencil(first_z, conductivity)
    partial_rz = jnp.sum(right_side * first_z, axis=(1, 2))
    partial_curvature = jnp.sum(first_z * applied, axis=(1, 2))
    extra = jnp.zeros((2, rank), jnp.float32)
    extra = extra.at[0, :2].set(partial_rz).at[1, :2].set(partial_curvature)
    spread, totals = sweep(project(applied), meets, extra, transfers, fronts)
    rz_old, curvature = totals[0, :2], totals[1, :2]
    step_size = rz_old / curvature
    mapped = leaf_apply(applied, leaf_inverse) + expand(spread)
    partial_square = jnp.sum(applied * mapped, axis=(1, 2))
    sent = jnp.broadcast_to(jnp.pad(partial_square, (0, rank - 2))[None], (meets.shape[0], rank))
    square = jnp.sum(lax.all_to_all(sent, AXES, 0, 0, tiled=True), axis=0)[:2]
    ratio = (step_size * square / curvature - 1.0)[:, None, None]
    step_size = step_size[:, None, None]
    solution = step_size * first_z
    residual = right_side - step_size * applied
    direction = first_z - step_size * mapped + ratio * first_z
    return (solution, residual, direction)


def solution(mesh):
    return jax.shard_map(
        on_device,
        mesh=mesh,
        in_specs=(
            P(None, "gx", "gy"),
            P("gx", "gy"),
            P("gx", "gy", None, None),
            P("gx", "gy", None),
            P("gx", "gy", None, None),
            P("gx", "gy", None, None, None),
            P("gx", "gy", None, None),
            P("gx", "gy", None, None, None),
        ),
        out_specs=(P(None, "gx", "gy"), P(None, "gx", "gy"), P(None, "gx", "gy")),
        check_vma=False,
    )
```

```python
from functools import partial

import jax
import jax.numpy as jnp
from jax import lax
from jax.experimental import pallas as pl
from jax.experimental.pallas import tpu as pltpu
from jax.sharding import PartitionSpec as P

LBX = 4
LBY = 32
AXES = ("gx", "gy")
F32 = jnp.float32
BF16 = jnp.bfloat16
VMEM_LIMIT = 12 << 20
PIECES = 4


ROWS = (((1,), (0,)), ((), ()))


def parts(value):
    high = value.astype(BF16)
    return high, (value - high.astype(F32)).astype(BF16)


def stacked(rows):
    high = rows.astype(BF16).astype(F32)
    rest = rows - high
    middle = rest.astype(BF16).astype(F32)
    return jnp.concatenate([high, middle, rest - middle], axis=0).astype(BF16)


def rows_times(rows, high, low):
    split = stacked(rows)
    count = rows.shape[0]
    total = lax.dot_general(split, low, ROWS, preferred_element_type=F32)
    total = total + lax.dot_general(split, high, ROWS, preferred_element_type=F32)
    return total[:count] + (total[count : 2 * count] + total[2 * count :])


def product(a, b):
    high, low = parts(b)
    left = jnp.concatenate(parts(a), axis=0)
    count = a.shape[0]
    total = lax.dot_general(left, low, ROWS, preferred_element_type=F32)
    total = total + lax.dot_general(left, high, ROWS, preferred_element_type=F32)
    return total[:count] + total[count:]


def in_vmem(*shape, dtype=F32):
    return pltpu.VMEM(shape, dtype)


def in_hbm(*shape, dtype=F32):
    return pltpu.HBM(shape, dtype)


def call(body, outs, arrays, flops, scratch=(), fetched=()):
    vmem = pl.BlockSpec(memory_space=pltpu.VMEM)
    hbm = pl.BlockSpec(memory_space=pltpu.HBM)
    size = sum(a.size * a.dtype.itemsize for a in arrays)
    fetched = [pltpu.with_memory_space_constraint(a, pltpu.HBM) for a in fetched]
    return pl.pallas_call(
        body,
        out_shape=tuple(outs),
        in_specs=[hbm] * len(fetched) + [vmem] * len(arrays),
        out_specs=(vmem,) * len(outs),
        scratch_shapes=scratch,
        compiler_params=pltpu.CompilerParams(vmem_limit_bytes=VMEM_LIMIT),
        cost_estimate=pl.CostEstimate(flops=flops, bytes_accessed=size, transcendentals=0),
    )(*fetched, *arrays)


def place():
    return lax.axis_index("gx") * lax.axis_size("gy") + lax.axis_index("gy")


def odd(axis):
    return lax.rem(lax.axis_index(axis), 2) == 1


def cousins(me, level):
    return ((me >> (level - 1)) ^ 1) << (level - 1)


def flat(ref):
    return jnp.concatenate([ref[:, x, :] for x in range(ref.shape[1])], axis=1)


def send_rows(sent, chain):
    me = place()
    count_s = chain[0].shape[0]
    for level in range(1, len(chain) + 1):
        size = 1 << (level - 1)
        rows = jnp.broadcast_to(chain[level - 1][None], (size,) + chain[level - 1].shape)
        sent[pl.ds(cousins(me, level), size), 0:count_s, :] = rows
    sent[me, 0:count_s, :] = jnp.zeros(chain[0].shape, F32)


def project_kernel(
    values_hbm, basis_hbm, leaf_hbm, node_hbm, conduct_hbm,
    sent, own, basis, wide_high, wide_low, transfers, values, conduct, sems,
):
    cells = basis.shape[0]
    piece = cells // PIECES
    copies = [pltpu.make_async_copy(values_hbm, values, sems.at[0])]
    for i in range(PIECES):
        at = pl.ds(i * piece, piece)
        copies.append(pltpu.make_async_copy(basis_hbm.at[at], basis.at[at], sems.at[1 + i]))
    copies.append(pltpu.make_async_copy(leaf_hbm, transfers.at[0], sems.at[1 + PIECES]))
    copies.append(pltpu.make_async_copy(node_hbm, transfers.at[pl.ds(1, node_hbm.shape[0])], sems.at[2 + PIECES]))
    copies.append(pltpu.make_async_copy(conduct_hbm, conduct, sems.at[3 + PIECES]))
    for copy in copies:
        copy.start()
    copies[0].wait()
    rows = flat(values)
    coeffs = jnp.zeros(own.shape, F32)
    for i in range(PIECES):
        copies[1 + i].wait()
        at = slice(i * piece, (i + 1) * piece)
        held = basis[at, :]
        coeffs = coeffs + rows_times(rows[:, at], *parts(held))
        wide_high[:, at], wide_low[:, at] = parts(held.T)
    own[...] = coeffs
    copies[1 + PIECES].wait()
    chain = [rows_times(coeffs, *parts(transfers[0]))]
    copies[2 + PIECES].wait()
    for h in range(1, transfers.shape[0]):
        chain.append(rows_times(chain[-1], *parts(transfers[h])))
    send_rows(sent, chain)
    copies[3 + PIECES].wait()


def window_kernel(
    inverse_hbm, leaf_hbm, node_hbm, values, transfers,
    near, up_high, up_low, down_high, down_low, inverse, fronts, held, sems,
):
    levels, rank = transfers.shape[0], transfers.shape[1]
    copies = [
        pltpu.make_async_copy(leaf_hbm, fronts.at[0], sems.at[0]),
        pltpu.make_async_copy(node_hbm, fronts.at[pl.ds(1, levels)], sems.at[1]),
        pltpu.make_async_copy(inverse_hbm, inverse, sems.at[2]),
    ]
    for copy in copies:
        copy.start()
    moves = [transfers[h] for h in range(levels)]
    back = [move.T for move in moves]
    ups, ups_t = [None, moves[0]], [None, back[0]]
    for h in range(1, levels):
        ups.append(product(ups[-1], moves[h]))
        ups_t.append(product(back[h], ups_t[-1]))
    for h in range(1, levels + 1):
        at = slice((h - 1) * rank, h * rank)
        up_high[:, at], up_low[:, at] = parts(ups[h])
    copies[0].wait()
    copies[1].wait()
    total = None
    for h in range(levels, -1, -1):
        front = fronts[h] if h == 0 else product(fronts[h], ups_t[h])
        total = front if total is None else front + product(moves[h], total)
        at = slice(h * rank, (h + 1) * rank)
        down_high[at, :], down_low[at, :] = parts(total)
    copies[2].wait()
    leaf_map(values, inverse, near, held)


def tree(got, own, down_high, down_low):
    me = place()
    count_s, rank = own.shape
    rows = [own[...]]
    for level in range(1, down_high.shape[0] // rank):
        size = 1 << (level - 1)
        rows.append(jnp.sum(got[pl.ds(cousins(me, level), size), 0:count_s, :], axis=0))
    return rows_times(jnp.concatenate(rows, axis=1), down_high[...], down_low[...])


def expand_into(out, spread, wide_high, wide_low, near):
    far = rows_times(spread, wide_high[...], wide_low[...])
    width = out.shape[2]
    for x in range(out.shape[1]):
        out[:, x, :] = near[:, x, :] + far[:, x * width : (x + 1) * width]


def edge_column(values, conduct, at):
    lane = lax.broadcasted_iota(jnp.int32, conduct.shape, 1)
    column = jnp.broadcast_to(conduct[:, at : at + 1], conduct.shape)
    for s in range(values.shape[0]):
        column = jnp.where(lane == s, jnp.broadcast_to(values[s, :, at : at + 1], conduct.shape), column)
    return column


def first_kernel(
    got, own, down_high, down_low, wide_high, wide_low, near, right, conduct,
    z, x_inner, x_outer, y_inner, y_outer, sums,
):
    expand_into(z, tree(got, own, down_high, down_low), wide_high, wide_low, near)
    count_s, extent_x, extent_y = z.shape
    odd_x, odd_y = odd("gx"), odd("gy")
    for s in range(count_s):
        head, tail = z[s, 0:1, :], z[s, extent_x - 1 : extent_x, :]
        x_inner[s : s + 1, :] = jnp.where(odd_x, head, tail)
        x_outer[s : s + 1, :] = jnp.where(odd_x, tail, head)
    head, tail = conduct[0:1, :], conduct[extent_x - 1 : extent_x, :]
    x_inner[count_s : count_s + 1, :] = jnp.where(odd_x, head, tail)
    x_outer[count_s : count_s + 1, :] = jnp.where(odd_x, tail, head)
    values, cond = z[...], conduct[...]
    head, tail = edge_column(values, cond, 0), edge_column(values, cond, extent_y - 1)
    y_inner[...] = jnp.where(odd_y, head, tail)
    y_outer[...] = jnp.where(odd_y, tail, head)
    sums[...] = jnp.sum(right[...] * values, axis=(1, 2))[:, None] * jnp.ones((1, extent_y), F32)


def second_kernel(
    x_inner, x_outer, y_inner, y_outer, z, conduct, basis, sums, up_high, up_low,
    applied, sent, own,
):
    count_s, extent_x, extent_y = z.shape
    odd_x, odd_y = odd("gx"), odd("gy")
    above = jnp.where(odd_x, x_inner[...], x_outer[...])
    below = jnp.where(odd_x, x_outer[...], x_inner[...])
    before = jnp.where(odd_y, y_inner[...], y_outer[...])
    after = jnp.where(odd_y, y_outer[...], y_inner[...])
    shape = (extent_x, extent_y)
    row = lax.broadcasted_iota(jnp.int32, shape, 0)
    lane = lax.broadcasted_iota(jnp.int32, shape, 1)

    def beside(field, at):
        down = jnp.where(row == extent_x - 1, below[at : at + 1, :], pltpu.roll(field, extent_x - 1, 0))
        up = jnp.where(row == 0, above[at : at + 1, :], pltpu.roll(field, 1, 0))
        right = jnp.where(lane == extent_y - 1, after[:, at : at + 1], pltpu.roll(field, extent_y - 1, 1))
        left = jnp.where(lane == 0, before[:, at : at + 1], pltpu.roll(field, 1, 1))
        return down, up, right, left

    cond = conduct[...]
    weights = [0.5 * (cond + other) for other in beside(cond, count_s)]
    lanes = lax.broadcasted_iota(jnp.int32, (1, extent_y), 1)
    packed = []
    for s in range(count_s):
        values = z[s]
        total = jnp.zeros(shape, F32)
        for weight, other in zip(weights, beside(values, s)):
            total = total + weight * (values - other)
        applied[s] = total
        curvature = jnp.sum(values * total)
        packed.append(jnp.where(lanes == 0, sums[s : s + 1, :], jnp.where(lanes == 1, curvature, 0.0)))
    coeffs = rows_times(flat(applied), *parts(basis[...]))
    own[...] = coeffs
    rank = coeffs.shape[1]
    chain = rows_times(coeffs, up_high[...], up_low[...])
    send_rows(sent, [chain[:, i : i + rank] for i in range(0, chain.shape[1], rank)])
    scalars = jnp.concatenate(packed, axis=0)
    sent[:, count_s:, :] = jnp.broadcast_to(scalars[None], (sent.shape[0],) + scalars.shape)


def third_kernel(got, own, down_high, down_low, near, applied, sent, spread, totals):
    count_s = own.shape[0]
    spread[...] = tree(got, own, down_high, down_low)
    totals[...] = jnp.sum(got[:, count_s:, :], axis=0)
    square = jnp.sum(near[...] * applied[...], axis=(1, 2)) + jnp.sum(own[...] * spread[...], axis=1)
    lanes = lax.broadcasted_iota(jnp.int32, (1, sent.shape[1]), 1)
    row = jnp.zeros((1, sent.shape[1]), F32)
    for s in range(count_s):
        row = jnp.where(lanes == s, square[s], row)
    sent[...] = jnp.broadcast_to(row, sent.shape)


def fourth_kernel(
    spread, totals, wide_high, wide_low, near, z, right, applied, solution, residual, partial_d, far
):
    expand_into(far, spread[...], wide_high, wide_low, near)
    for s in range(z.shape[0]):
        step = totals[s : s + 1, 0:1] / totals[s : s + 1, 1:2]
        solution[s] = step * z[s]
        residual[s] = right[s] - step * applied[s]
        partial_d[s] = z[s] - step * far[s]


def fifth_kernel(got, totals, z, partial_d, direction):
    square = jnp.sum(got[...], axis=0, keepdims=True)
    for s in range(z.shape[0]):
        curvature = totals[s : s + 1, 1:2]
        step = totals[s : s + 1, 0:1] / curvature
        ratio = step * square[0:1, s : s + 1] / curvature - 1.0
        direction[s] = partial_d[s] + ratio * z[s]


def leaf_kernel(inverse_hbm, values, out, inverse, held, sem):
    copy = pltpu.make_async_copy(inverse_hbm, inverse, sem)
    copy.start()
    copy.wait()
    leaf_map(values, inverse, out, held)


def leaf_map(values, inverse, out, held):
    count_s, extent_x, extent_y = values.shape
    blocks_x, blocks_y = extent_x // LBX, extent_y // LBY
    rows = count_s * blocks_x
    group = lax.broadcasted_iota(jnp.int32, (rows, extent_y), 1) // LBY
    owner = lax.rem(lax.broadcasted_iota(jnp.int32, (rows, extent_y), 0), blocks_x)

    def regroup(lines):
        outs = []
        for q in range(len(lines)):
            out_q = lines[q]
            for a in range(len(lines)):
                if a != q:
                    turned = pltpu.roll(lines[a], ((a - q) * LBY) % extent_y, 1)
                    out_q = jnp.where(group == a, turned, out_q)
            outs.append(out_q)
        return outs

    lines = [
        jnp.concatenate(
            [values[s, p * LBX + a : p * LBX + a + 1, :] for s in range(count_s) for p in range(blocks_x)], axis=0
        )
        for a in range(LBX)
    ]
    mapped = []
    for q, block in enumerate(regroup(lines)):
        wide = jnp.concatenate([jnp.where(owner == p, block, 0.0) for p in range(blocks_x)], axis=1)
        stack = jnp.concatenate([inverse[p, q] for p in range(blocks_x)], axis=0)
        mapped.append(rows_times(wide, *parts(stack)))
    for a, line in enumerate(regroup(mapped)):
        held[a] = line
    for s in range(count_s):
        for p in range(blocks_x):
            for a in range(LBX):
                out[s, p * LBX + a : p * LBX + a + 1, :] = held[a, s * blocks_x + p : s * blocks_x + p + 1, :]


def pair_exchange(inner_value, outer_value, axis):
    count = lax.axis_size(axis)
    inner = [(i, i ^ 1) for i in range(count)]
    outer = []
    for i in range(1, count - 1, 2):
        outer += [(i, i + 1), (i + 1, i)]
    return lax.ppermute(inner_value, axis, inner), lax.ppermute(outer_value, axis, outer)


def on_device(
    right_side,
    conductivity,
    leaf_inverse,
    front_basis,
    leaf_transfer,
    node_transfer,
    leaf_front,
    node_front,
):
    levels = node_front.shape[2]
    count = 1 << levels
    count_s, extent_x, extent_y = right_side.shape
    rank = front_basis.shape[-1]
    basis = front_basis.reshape(extent_x * extent_y, rank)
    leaf_t, node_t = leaf_transfer[0, 0], node_transfer[0, 0]
    leaf_f, node_f = leaf_front[0, 0], node_front[0, 0]
    field = (count_s, extent_x, extent_y)
    cells = extent_x * extent_y

    def pair(*shape):
        return (in_vmem(*shape, dtype=BF16),) * 2

    sent, own, basis, wide_high, wide_low, transfers, right_side, conductivity = call(
        project_kernel,
        (
            in_hbm(count, count_s, rank),
            in_vmem(count_s, rank),
            in_vmem(cells, rank),
            *pair(rank, cells),
            in_vmem(levels, rank, rank),
            in_vmem(*field),
            in_vmem(extent_x, extent_y),
        ),
        (),
        10**6,
        (pltpu.SemaphoreType.DMA((4 + PIECES,)),),
        (right_side, basis, leaf_t, node_t, conductivity),
    )
    got = lax.all_to_all(sent, AXES, 0, 0)
    blocks = leaf_inverse.shape
    held = pltpu.VMEM((LBX, count_s * extent_x // LBX, extent_y), F32)
    near, up_high, up_low, down_high, down_low = call(
        window_kernel,
        (in_vmem(*field), *pair(rank, levels * rank), *pair((levels + 1) * rank, rank)),
        (right_side, transfers),
        10**7,
        (pltpu.VMEM(blocks, F32), pltpu.VMEM((levels + 1, rank, rank), F32), held, pltpu.SemaphoreType.DMA((3,))),
        (leaf_inverse, leaf_f, node_f),
    )
    edge = (count_s + 1, extent_y)
    first_z, x_inner, x_outer, y_inner, y_outer, sums = call(
        first_kernel,
        [in_vmem(*s) for s in (field, edge, edge, (extent_x, extent_y), (extent_x, extent_y), (count_s, extent_y))],
        (got, own, down_high, down_low, wide_high, wide_low, near, right_side, conductivity),
        10**6,
    )
    x_inner, x_outer = pair_exchange(x_inner, x_outer, "gx")
    y_inner, y_outer = pair_exchange(y_inner, y_outer, "gy")
    applied, sent, own = call(
        second_kernel,
        (in_vmem(*field), in_hbm(count, 2 * count_s, rank), in_vmem(count_s, rank)),
        (x_inner, x_outer, y_inner, y_outer, first_z, conductivity, basis, sums, up_high, up_low),
        10**6,
    )
    got = lax.all_to_all(sent, AXES, 0, 0)
    (near,) = call(
        leaf_kernel,
        (in_vmem(*field),),
        (applied,),
        10**7,
        (pltpu.VMEM(blocks, F32), held, pltpu.SemaphoreType.DMA(())),
        (leaf_inverse,),
    )
    sent, spread, totals = call(
        third_kernel,
        (in_hbm(count, rank), in_vmem(count_s, rank), in_vmem(count_s, rank)),
        (got, own, down_high, down_low, near, applied),
        10**6,
    )
    got = lax.all_to_all(sent, AXES, 0, 0, tiled=True)
    solution, residual, partial_d = call(
        fourth_kernel,
        (in_hbm(*field), in_hbm(*field), in_vmem(*field)),
        (spread, totals, wide_high, wide_low, near, first_z, right_side, applied),
        10**7,
        (pltpu.VMEM(field, F32),),
    )
    (direction,) = call(fifth_kernel, (in_hbm(*field),), (got, totals, first_z, partial_d), 10**6)
    return (solution, residual, direction)


def solution(mesh):
    return jax.shard_map(
        on_device,
        mesh=mesh,
        in_specs=(
            P(None, "gx", "gy"),
            P("gx", "gy"),
            P("gx", "gy", None, None),
            P("gx", "gy", None),
            P("gx", "gy", None, None),
            P("gx", "gy", None, None, None),
            P("gx", "gy", None, None),
            P("gx", "gy", None, None, None),
        ),
        out_specs=(P(None, "gx", "gy"), P(None, "gx", "gy"), P(None, "gx", "gy")),
        check_vma=False,
    )
```

```python
import jax
import jax.numpy as jnp
from jax import lax
from jax.experimental import pallas as pl
from jax.experimental.pallas import tpu as pltpu
from jax.sharding import PartitionSpec as P

LBX = 4
LBY = 32
AXES = ("gx", "gy")
F32 = jnp.float32
BF16 = jnp.bfloat16
VMEM_LIMIT = 12 << 20
PIECES = 4


ROWS = (((1,), (0,)), ((), ()))
LANES = (((1,), (1,)), ((), ()))


def parts(value):
    high = value.astype(BF16)
    return high, (value - high.astype(F32)).astype(BF16)


def stacked(rows):
    high = rows.astype(BF16).astype(F32)
    rest = rows - high
    middle = rest.astype(BF16).astype(F32)
    return jnp.concatenate([high, middle, rest - middle], axis=0).astype(BF16)


def rows_times(rows, high, low, dims=ROWS):
    split = stacked(rows)
    count = rows.shape[0]
    total = lax.dot_general(split, low, dims, preferred_element_type=F32)
    total = total + lax.dot_general(split, high, dims, preferred_element_type=F32)
    return total[:count] + (total[count : 2 * count] + total[2 * count :])


def product(a, b):
    high, low = parts(b)
    left = jnp.concatenate(parts(a), axis=0)
    count = a.shape[0]
    total = lax.dot_general(left, low, ROWS, preferred_element_type=F32)
    total = total + lax.dot_general(left, high, ROWS, preferred_element_type=F32)
    return total[:count] + total[count:]


def in_vmem(*shape, dtype=F32):
    return pltpu.VMEM(shape, dtype)


def in_hbm(*shape, dtype=F32):
    return pltpu.HBM(shape, dtype)


def call(body, outs, arrays, flops, scratch=(), fetched=(), written=False):
    vmem = pl.BlockSpec(memory_space=pltpu.VMEM)
    hbm = pl.BlockSpec(memory_space=pltpu.HBM)
    size = sum(a.size * a.dtype.itemsize for a in arrays)
    fetched = [pltpu.with_memory_space_constraint(a, pltpu.HBM) for a in fetched]
    return pl.pallas_call(
        body,
        out_shape=tuple(outs),
        in_specs=[hbm] * len(fetched) + [vmem] * len(arrays),
        out_specs=(hbm if written else vmem,) * len(outs),
        scratch_shapes=scratch,
        compiler_params=pltpu.CompilerParams(vmem_limit_bytes=VMEM_LIMIT),
        cost_estimate=pl.CostEstimate(flops=flops, bytes_accessed=size, transcendentals=0),
    )(*fetched, *arrays)


def place():
    return lax.axis_index("gx") * lax.axis_size("gy") + lax.axis_index("gy")


def odd(axis):
    return lax.rem(lax.axis_index(axis), 2) == 1


def cousins(me, level):
    return ((me >> (level - 1)) ^ 1) << (level - 1)


def flat(ref):
    return jnp.concatenate([ref[:, x, :] for x in range(ref.shape[1])], axis=1)


def send_rows(sent, chain):
    me = place()
    count_s = chain[0].shape[0]
    for level in range(1, len(chain) + 1):
        size = 1 << (level - 1)
        rows = jnp.broadcast_to(chain[level - 1][None], (size,) + chain[level - 1].shape)
        sent[pl.ds(cousins(me, level), size), 0:count_s, :] = rows
    sent[me, 0:count_s, :] = jnp.zeros(chain[0].shape, F32)


def project_kernel(
    leaf_t, node_t, values_hbm, basis_hbm, conduct_hbm,
    sent, own, wide_high, wide_low, up_high, up_low, moves, values, conduct, basis, sems,
):
    levels, rank = moves.shape[0], moves.shape[1]
    piece = basis.shape[0] // PIECES
    pairs = [(values_hbm, values), (leaf_t, moves.at[0]), (node_t, moves.at[pl.ds(1, levels - 1)])]
    pairs += [(basis_hbm.at[pl.ds(i * piece, piece)], basis.at[pl.ds(i * piece, piece)]) for i in range(PIECES)]
    pairs += [(conduct_hbm, conduct)]
    copies = [pltpu.make_async_copy(source, target, sems.at[i]) for i, (source, target) in enumerate(pairs)]
    for copy in copies:
        copy.start()
    for copy in copies[:3]:
        copy.wait()
    rows = flat(values)
    coeffs = jnp.zeros(own.shape, F32)
    up = moves[0]
    up_high[:, 0:rank], up_low[:, 0:rank] = parts(up)
    for i in range(max(PIECES, levels - 1)):
        if i < PIECES:
            copies[3 + i].wait()
            at = slice(i * piece, (i + 1) * piece)
            held = basis[at, :]
            coeffs = coeffs + rows_times(rows[:, at], *parts(held))
            wide_high[:, at], wide_low[:, at] = parts(held.T)
        if i + 1 < levels:
            up = product(up, moves[i + 1])
            at = slice((i + 1) * rank, (i + 2) * rank)
            up_high[:, at], up_low[:, at] = parts(up)
    own[...] = coeffs
    send_chain(sent, coeffs, up_high, up_low)
    copies[3 + PIECES].wait()


def send_chain(sent, coeffs, up_high, up_low):
    rank = coeffs.shape[1]
    chain = rows_times(coeffs, up_high[...], up_low[...])
    send_rows(sent, [chain[:, i : i + rank] for i in range(0, chain.shape[1], rank)])


def window_kernel(
    leaf_f, node_f, inverse_hbm, values, moves, up_high, up_low,
    near, down_high, down_low, inverse, fronts, held, sems,
):
    levels, rank = moves.shape[0], moves.shape[1]
    copies = [
        pltpu.make_async_copy(leaf_f, fronts.at[0], sems.at[0]),
        pltpu.make_async_copy(node_f, fronts.at[pl.ds(1, levels)], sems.at[1]),
        pltpu.make_async_copy(inverse_hbm, inverse, sems.at[2]),
    ]
    for copy in copies:
        copy.start()
    columns = [slice(h * rank, (h + 1) * rank) for h in range(levels + 1)]
    back = [(up_high[:, at].astype(F32) + up_low[:, at].astype(F32)).T for at in columns[:levels]]
    copies[0].wait()
    copies[1].wait()
    total = [fronts[0]] + [product(fronts[h + 1], back[h]) for h in range(levels)]
    copies[2].wait()
    for h in range(levels, -1, -1):
        if h < levels:
            total[h] = total[h] + product(moves[h], total[h + 1])
        down_high[columns[h], :], down_low[columns[h], :] = parts(total[h])
    leaf_map(values, inverse, near, held)


def tree(got, own, down_high, down_low):
    me = place()
    count_s, rank = own.shape
    rows = [own[...]]
    for level in range(1, down_high.shape[0] // rank):
        size = 1 << (level - 1)
        rows.append(jnp.sum(got[pl.ds(cousins(me, level), size), 0:count_s, :], axis=0))
    return rows_times(jnp.concatenate(rows, axis=1), down_high[...], down_low[...])


def expand_into(out, spread, wide_high, wide_low, near):
    far = rows_times(spread, wide_high[...], wide_low[...])
    width = out.shape[2]
    for x in range(out.shape[1]):
        out[:, x, :] = near[:, x, :] + far[:, x * width : (x + 1) * width]


def edge_column(values, conduct, at):
    lane = lax.broadcasted_iota(jnp.int32, conduct.shape, 1)
    column = jnp.broadcast_to(conduct[:, at : at + 1], conduct.shape)
    for s in range(values.shape[0]):
        column = jnp.where(lane == s, jnp.broadcast_to(values[s, :, at : at + 1], conduct.shape), column)
    return column


def first_kernel(
    got, own, down_high, down_low, wide_high, wide_low, near, right, conduct,
    z, x_inner, x_outer, y_inner, y_outer, sums,
):
    expand_into(z, tree(got, own, down_high, down_low), wide_high, wide_low, near)
    count_s, extent_x, extent_y = z.shape
    odd_x, odd_y = odd("gx"), odd("gy")
    for s in range(count_s):
        head, tail = z[s, 0:1, :], z[s, extent_x - 1 : extent_x, :]
        x_inner[s : s + 1, :] = jnp.where(odd_x, head, tail)
        x_outer[s : s + 1, :] = jnp.where(odd_x, tail, head)
    head, tail = conduct[0:1, :], conduct[extent_x - 1 : extent_x, :]
    x_inner[count_s : count_s + 1, :] = jnp.where(odd_x, head, tail)
    x_outer[count_s : count_s + 1, :] = jnp.where(odd_x, tail, head)
    values, cond = z[...], conduct[...]
    head, tail = edge_column(values, cond, 0), edge_column(values, cond, extent_y - 1)
    y_inner[...] = jnp.where(odd_y, head, tail)
    y_outer[...] = jnp.where(odd_y, tail, head)
    sums[...] = jnp.sum(right[...] * values, axis=(1, 2))[:, None] * jnp.ones((1, extent_y), F32)


def second_kernel(
    x_inner, x_outer, y_inner, y_outer, z, conduct, wide_high, wide_low, sums, up_high, up_low, inverse,
    applied, near, sent, own, held,
):
    count_s, extent_x, extent_y = z.shape
    odd_x, odd_y = odd("gx"), odd("gy")
    above = jnp.where(odd_x, x_inner[...], x_outer[...])
    below = jnp.where(odd_x, x_outer[...], x_inner[...])
    before = jnp.where(odd_y, y_inner[...], y_outer[...])
    after = jnp.where(odd_y, y_outer[...], y_inner[...])
    shape = (extent_x, extent_y)
    row = lax.broadcasted_iota(jnp.int32, shape, 0)
    lane = lax.broadcasted_iota(jnp.int32, shape, 1)

    def beside(field, at):
        down = jnp.where(row == extent_x - 1, below[at : at + 1, :], pltpu.roll(field, extent_x - 1, 0))
        up = jnp.where(row == 0, above[at : at + 1, :], pltpu.roll(field, 1, 0))
        right = jnp.where(lane == extent_y - 1, after[:, at : at + 1], pltpu.roll(field, extent_y - 1, 1))
        left = jnp.where(lane == 0, before[:, at : at + 1], pltpu.roll(field, 1, 1))
        return down, up, right, left

    cond = conduct[...]
    weights = [0.5 * (cond + other) for other in beside(cond, count_s)]
    lanes = lax.broadcasted_iota(jnp.int32, (1, extent_y), 1)
    packed = []
    for s in range(count_s):
        values = z[s]
        total = jnp.zeros(shape, F32)
        for weight, other in zip(weights, beside(values, s)):
            total = total + weight * (values - other)
        applied[s] = total
        curvature = jnp.sum(values * total)
        packed.append(jnp.where(lanes == 0, sums[s : s + 1, :], jnp.where(lanes == 1, curvature, 0.0)))
    coeffs = rows_times(flat(applied), wide_high[...], wide_low[...], LANES)
    own[...] = coeffs
    send_chain(sent, coeffs, up_high, up_low)
    scalars = jnp.concatenate(packed, axis=0)
    sent[:, count_s:, :] = jnp.broadcast_to(scalars[None], (sent.shape[0],) + scalars.shape)
    leaf_map(applied, inverse, near, held)


def third_kernel(
    got, own, down_high, down_low, wide_high, wide_low, near, z, right, applied,
    sent, totals, solution, residual, partial_d, far,
):
    count_s = own.shape[0]
    spread = tree(got, own, down_high, down_low)
    scalars = jnp.sum(got[:, count_s:, :], axis=0)
    totals[...] = scalars
    square = jnp.sum(near[...] * applied[...], axis=(1, 2)) + jnp.sum(own[...] * spread, axis=1)
    lanes = lax.broadcasted_iota(jnp.int32, (1, sent.shape[1]), 1)
    row = jnp.zeros((1, sent.shape[1]), F32)
    for s in range(count_s):
        row = jnp.where(lanes == s, square[s], row)
    sent[...] = jnp.broadcast_to(row, sent.shape)
    expand_into(far, spread, wide_high, wide_low, near)
    for s in range(count_s):
        step = scalars[s : s + 1, 0:1] / scalars[s : s + 1, 1:2]
        solution[s] = step * z[s]
        residual[s] = right[s] - step * applied[s]
        partial_d[s] = z[s] - step * far[s]


def last_kernel(got, totals, z, partial_d, solution, residual, solution_hbm, residual_hbm, direction_hbm, direction, sems):
    copies = [
        pltpu.make_async_copy(solution, solution_hbm, sems.at[0]),
        pltpu.make_async_copy(residual, residual_hbm, sems.at[1]),
        pltpu.make_async_copy(direction, direction_hbm, sems.at[2]),
    ]
    copies[0].start()
    copies[1].start()
    square = jnp.sum(got[...], axis=0, keepdims=True)
    for s in range(z.shape[0]):
        curvature = totals[s : s + 1, 1:2]
        step = totals[s : s + 1, 0:1] / curvature
        ratio = step * square[0:1, s : s + 1] / curvature - 1.0
        direction[s] = partial_d[s] + ratio * z[s]
    copies[2].start()
    for copy in copies:
        copy.wait()


def leaf_map(values, inverse, out, held):
    count_s, extent_x, extent_y = values.shape
    blocks_x = extent_x // LBX
    rows = count_s * blocks_x
    group = lax.broadcasted_iota(jnp.int32, (rows, extent_y), 1) // LBY
    owner = lax.rem(lax.broadcasted_iota(jnp.int32, (rows, extent_y), 0), blocks_x)

    def regroup(lines):
        outs = []
        for q in range(len(lines)):
            out_q = lines[q]
            for a in range(len(lines)):
                if a != q:
                    turned = pltpu.roll(lines[a], ((a - q) * LBY) % extent_y, 1)
                    out_q = jnp.where(group == a, turned, out_q)
            outs.append(out_q)
        return outs

    lines = [
        jnp.concatenate(
            [values[s, p * LBX + a : p * LBX + a + 1, :] for s in range(count_s) for p in range(blocks_x)], axis=0
        )
        for a in range(LBX)
    ]
    mapped = []
    for q, block in enumerate(regroup(lines)):
        wide = jnp.concatenate([jnp.where(owner == p, block, 0.0) for p in range(blocks_x)], axis=1)
        stack = jnp.concatenate([inverse[p, q] for p in range(blocks_x)], axis=0)
        mapped.append(rows_times(wide, *parts(stack)))
    for a, line in enumerate(regroup(mapped)):
        held[a] = line
    for s in range(count_s):
        for p in range(blocks_x):
            for a in range(LBX):
                out[s, p * LBX + a : p * LBX + a + 1, :] = held[a, s * blocks_x + p : s * blocks_x + p + 1, :]


def pair_exchange(inner_value, outer_value, axis):
    count = lax.axis_size(axis)
    inner = [(i, i ^ 1) for i in range(count)]
    outer = []
    for i in range(1, count - 1, 2):
        outer += [(i, i + 1), (i + 1, i)]
    inner_value = lax.ppermute(inner_value, axis, inner)
    outer_value = lax.ppermute(outer_value, axis, outer)
    return inner_value, outer_value


def on_device(
    right_side,
    conductivity,
    leaf_inverse,
    front_basis,
    leaf_transfer,
    node_transfer,
    leaf_front,
    node_front,
):
    levels = node_front.shape[2]
    count = 1 << levels
    count_s, extent_x, extent_y = right_side.shape
    rank = front_basis.shape[-1]
    basis = front_basis.reshape(extent_x * extent_y, rank)
    leaf_t, node_t = leaf_transfer[0, 0], node_transfer[0, 0]
    leaf_f, node_f = leaf_front[0, 0], node_front[0, 0]
    field = (count_s, extent_x, extent_y)
    cells = extent_x * extent_y

    def pair(*shape):
        return (in_vmem(*shape, dtype=BF16),) * 2

    sent, own, wide_high, wide_low, up_high, up_low, moves, right_side, conductivity = call(
        project_kernel,
        (
            in_hbm(count, count_s, rank),
            in_vmem(count_s, rank),
            *pair(rank, cells),
            *pair(rank, levels * rank),
            in_vmem(levels, rank, rank),
            in_vmem(*field),
            in_vmem(extent_x, extent_y),
        ),
        (),
        10**6,
        (pltpu.VMEM((cells, rank), F32), pltpu.SemaphoreType.DMA((4 + PIECES,))),
        (leaf_t, node_t, right_side, basis, conductivity),
    )
    got = lax.all_to_all(sent, AXES, 0, 0)
    held = pltpu.VMEM((LBX, count_s * extent_x // LBX, extent_y), F32)
    near, down_high, down_low, inverse = call(
        window_kernel,
        (in_vmem(*field), *pair((levels + 1) * rank, rank), in_vmem(*leaf_inverse.shape)),
        (right_side, moves, up_high, up_low),
        10**7,
        (pltpu.VMEM((levels + 1, rank, rank), F32), held, pltpu.SemaphoreType.DMA((3,))),
        (leaf_f, node_f, leaf_inverse),
    )
    edge = (count_s + 1, extent_y)
    first_z, x_inner, x_outer, y_inner, y_outer, sums = call(
        first_kernel,
        [in_vmem(*s) for s in (field, edge, edge, (extent_x, extent_y), (extent_x, extent_y), (count_s, extent_y))],
        (got, own, down_high, down_low, wide_high, wide_low, near, right_side, conductivity),
        10**6,
    )
    x_inner, x_outer = pair_exchange(x_inner, x_outer, "gx")
    y_inner, y_outer = pair_exchange(y_inner, y_outer, "gy")
    applied, near, sent, own = call(
        second_kernel,
        (in_vmem(*field), in_vmem(*field), in_vmem(count, 2 * count_s, rank), in_vmem(count_s, rank)),
        (x_inner, x_outer, y_inner, y_outer, first_z, conductivity, wide_high, wide_low, sums, up_high, up_low, inverse),
        10**6,
        (held,),
    )
    got = lax.all_to_all(sent, AXES, 0, 0)
    sent, totals, step_z, residual, partial_d = call(
        third_kernel,
        (in_vmem(count, rank), in_vmem(count_s, rank), in_vmem(*field), in_vmem(*field), in_vmem(*field)),
        (got, own, down_high, down_low, wide_high, wide_low, near, first_z, right_side, applied),
        10**6,
        (pltpu.VMEM(field, F32),),
    )
    got = lax.all_to_all(sent, AXES, 0, 0, tiled=True)
    return call(
        last_kernel,
        (in_hbm(*field),) * 3,
        (got, totals, first_z, partial_d, step_z, residual),
        10**6,
        (pltpu.VMEM(field, F32), pltpu.SemaphoreType.DMA((3,))),
        written=True,
    )


def solution(mesh):
    return jax.shard_map(
        on_device,
        mesh=mesh,
        in_specs=(
            P(None, "gx", "gy"),
            P("gx", "gy"),
            P("gx", "gy", None, None),
            P("gx", "gy", None),
            P("gx", "gy", None, None),
            P("gx", "gy", None, None, None),
            P("gx", "gy", None, None),
            P("gx", "gy", None, None, None),
        ),
        out_specs=(P(None, "gx", "gy"), P(None, "gx", "gy"), P(None, "gx", "gy")),
        check_vma=False,
    )
```

```python
import jax
import jax.numpy as jnp
from jax import lax
from jax.experimental import pallas as pl
from jax.experimental.pallas import tpu as pltpu
from jax.sharding import PartitionSpec as P

LBX = 4
LBY = 32
AXES = ("gx", "gy")
F32 = jnp.float32
BF16 = jnp.bfloat16
VMEM_LIMIT = 12 << 20
PIECES = 2


ROWS = (((1,), (0,)), ((), ()))
LANES = (((1,), (1,)), ((), ()))


def parts(value):
    high = value.astype(BF16)
    return high, (value - high.astype(F32)).astype(BF16)


def stacked(rows):
    high = rows.astype(BF16).astype(F32)
    rest = rows - high
    middle = rest.astype(BF16).astype(F32)
    return jnp.concatenate([high, middle, rest - middle], axis=0).astype(BF16)


def rows_times(rows, high, low, dims=ROWS):
    split = stacked(rows)
    count = rows.shape[0]
    total = lax.dot_general(split, low, dims, preferred_element_type=F32)
    total = total + lax.dot_general(split, high, dims, preferred_element_type=F32)
    return total[:count] + (total[count : 2 * count] + total[2 * count :])


def product(a, b):
    high, low = parts(b)
    left = jnp.concatenate(parts(a), axis=0)
    count = a.shape[0]
    total = lax.dot_general(left, low, ROWS, preferred_element_type=F32)
    total = total + lax.dot_general(left, high, ROWS, preferred_element_type=F32)
    return total[:count] + total[count:]


def in_vmem(*shape, dtype=F32):
    return pltpu.VMEM(shape, dtype)


def in_hbm(*shape, dtype=F32):
    return pltpu.HBM(shape, dtype)


def call(body, outs, arrays, flops, scratch=(), fetched=(), written=0):
    vmem = pl.BlockSpec(memory_space=pltpu.VMEM)
    hbm = pl.BlockSpec(memory_space=pltpu.HBM)
    size = sum(a.size * a.dtype.itemsize for a in arrays)
    fetched = [pltpu.with_memory_space_constraint(a, pltpu.HBM) for a in fetched]
    return pl.pallas_call(
        body,
        out_shape=tuple(outs),
        in_specs=[hbm] * len(fetched) + [vmem] * len(arrays),
        out_specs=(hbm,) * written + (vmem,) * (len(outs) - written),
        scratch_shapes=scratch,
        compiler_params=pltpu.CompilerParams(vmem_limit_bytes=VMEM_LIMIT),
        cost_estimate=pl.CostEstimate(flops=flops, bytes_accessed=size, transcendentals=0),
    )(*fetched, *arrays)


def place():
    return lax.axis_index("gx") * lax.axis_size("gy") + lax.axis_index("gy")


def odd(axis):
    return lax.rem(lax.axis_index(axis), 2) == 1


def cousins(me, level):
    return ((me >> (level - 1)) ^ 1) << (level - 1)


def flat(ref):
    return jnp.concatenate([ref[:, x, :] for x in range(ref.shape[1])], axis=1)


def send_rows(sent, chain):
    me = place()
    count_s = chain[0].shape[0]
    for level in range(1, len(chain) + 1):
        size = 1 << (level - 1)
        rows = jnp.broadcast_to(chain[level - 1][None], (size,) + chain[level - 1].shape)
        sent[pl.ds(cousins(me, level), size), 0:count_s, :] = rows
    sent[me, 0:count_s, :] = jnp.zeros(chain[0].shape, F32)


def project_kernel(
    leaf_t, node_t, values_hbm, basis_hbm, conduct_hbm,
    sent_hbm, own, wide_high, wide_low, up_high, up_low, moves, values, conduct, basis, sent, sems,
):
    levels, rank = moves.shape[0], moves.shape[1]
    piece = basis.shape[0] // PIECES
    slabs = [slice(i * piece, (i + 1) * piece) for i in range(PIECES)]
    pairs = [(leaf_t, moves.at[0]), (node_t, moves.at[pl.ds(1, levels - 1)]), (values_hbm, values)]
    pairs += [(basis_hbm.at[pl.ds(i * piece, piece)], basis.at[pl.ds(i * piece, piece)]) for i in range(PIECES)]
    pairs += [(conduct_hbm, conduct), (sent, sent_hbm)]
    copies = [pltpu.make_async_copy(source, target, sems.at[i]) for i, (source, target) in enumerate(pairs)]
    for copy in copies[:-1]:
        copy.start()
    copies[2].wait()
    rows = flat(values)
    coeffs = jnp.zeros(own.shape, F32)
    copies[0].wait()
    copies[1].wait()
    ups = [moves[0]]
    both = [product(moves[h], moves[h + 1]) for h in range(0, levels - 1, 2)]
    waiting = list(enumerate(slabs))
    while len(ups) < levels:
        h = len(ups) - 1
        if h % 2 == 0:
            ups.append(product(ups[h - 1], both[h // 2]) if h else both[0])
            if waiting:
                i, at = waiting.pop(0)
                copies[3 + i].wait()
                coeffs = coeffs + rows_times(rows[:, at], *parts(basis[at, :]))
        else:
            ups.append(product(ups[h], moves[h + 1]))
    for i, at in waiting:
        copies[3 + i].wait()
        coeffs = coeffs + rows_times(rows[:, at], *parts(basis[at, :]))
    for h in range(levels):
        at = slice(h * rank, (h + 1) * rank)
        up_high[:, at], up_low[:, at] = parts(ups[h])
    own[...] = coeffs
    send_chain(sent, coeffs, up_high, up_low)
    copies[-1].start()
    for at in slabs:
        wide_high[:, at], wide_low[:, at] = parts(basis[at, :].T)
    copies[-2].wait()
    copies[-1].wait()


def send_chain(sent, coeffs, up_high, up_low):
    rank = coeffs.shape[1]
    chain = rows_times(coeffs, up_high[...], up_low[...])
    send_rows(sent, [chain[:, i : i + rank] for i in range(0, chain.shape[1], rank)])


def window_kernel(
    leaf_f, node_f, inverse_hbm, values, moves, up_high, up_low,
    near, down_high, down_low, inverse, fronts, held, sems,
):
    levels, rank = moves.shape[0], moves.shape[1]
    copies = [
        pltpu.make_async_copy(leaf_f, fronts.at[0], sems.at[0]),
        pltpu.make_async_copy(node_f, fronts.at[pl.ds(1, levels)], sems.at[1]),
        pltpu.make_async_copy(inverse_hbm, inverse, sems.at[2]),
    ]
    for copy in copies:
        copy.start()
    columns = [slice(h * rank, (h + 1) * rank) for h in range(levels + 1)]
    back = [(up_high[:, at].astype(F32) + up_low[:, at].astype(F32)).T for at in columns[:levels]]
    copies[0].wait()
    copies[1].wait()
    total = [fronts[0]] + [product(fronts[h + 1], back[h]) for h in range(levels)]
    for h in range(levels, -1, -1):
        if h == levels // 2:
            copies[2].wait()
            leaf_map(values, inverse, near, held)
        if h < levels:
            total[h] = total[h] + product(moves[h], total[h + 1])
        down_high[columns[h], :], down_low[columns[h], :] = parts(total[h])


def tree(got, own, down_high, down_low):
    me = place()
    count_s, rank = own.shape
    rows = [own[...]]
    for level in range(1, down_high.shape[0] // rank):
        size = 1 << (level - 1)
        rows.append(jnp.sum(got[pl.ds(cousins(me, level), size), 0:count_s, :], axis=0))
    return rows_times(jnp.concatenate(rows, axis=1), down_high[...], down_low[...])


def expand_into(out, spread, wide_high, wide_low, near):
    far = rows_times(spread, wide_high[...], wide_low[...])
    width = out.shape[2]
    for x in range(out.shape[1]):
        out[:, x, :] = near[:, x, :] + far[:, x * width : (x + 1) * width]


def edge_column(values, conduct, at):
    lane = lax.broadcasted_iota(jnp.int32, conduct.shape, 1)
    column = jnp.broadcast_to(conduct[:, at : at + 1], conduct.shape)
    for s in range(values.shape[0]):
        column = jnp.where(lane == s, jnp.broadcast_to(values[s, :, at : at + 1], conduct.shape), column)
    return column


def first_kernel(
    got, own, down_high, down_low, wide_high, wide_low, near, right, conduct,
    z, x_inner, x_outer, y_inner, y_outer, sums,
):
    expand_into(z, tree(got, own, down_high, down_low), wide_high, wide_low, near)
    count_s, extent_x, extent_y = z.shape
    odd_x, odd_y = odd("gx"), odd("gy")
    for s in range(count_s):
        head, tail = z[s, 0:1, :], z[s, extent_x - 1 : extent_x, :]
        x_inner[s : s + 1, :] = jnp.where(odd_x, head, tail)
        x_outer[s : s + 1, :] = jnp.where(odd_x, tail, head)
    head, tail = conduct[0:1, :], conduct[extent_x - 1 : extent_x, :]
    x_inner[count_s : count_s + 1, :] = jnp.where(odd_x, head, tail)
    x_outer[count_s : count_s + 1, :] = jnp.where(odd_x, tail, head)
    values, cond = z[...], conduct[...]
    head, tail = edge_column(values, cond, 0), edge_column(values, cond, extent_y - 1)
    y_inner[...] = jnp.where(odd_y, head, tail)
    y_outer[...] = jnp.where(odd_y, tail, head)
    for s in range(count_s):
        sums[s : s + 1, :] = jnp.broadcast_to(jnp.sum(right[s] * values[s]), (1, extent_y))


def second_kernel(
    x_inner, x_outer, y_inner, y_outer, z, conduct, wide_high, wide_low, up_high, up_low, inverse,
    applied, near, sent, own, curvature, held,
):
    count_s, extent_x, extent_y = z.shape
    odd_x, odd_y = odd("gx"), odd("gy")
    above = jnp.where(odd_x, x_inner[...], x_outer[...])
    below = jnp.where(odd_x, x_outer[...], x_inner[...])
    before = jnp.where(odd_y, y_inner[...], y_outer[...])
    after = jnp.where(odd_y, y_outer[...], y_inner[...])
    shape = (extent_x, extent_y)
    row = lax.broadcasted_iota(jnp.int32, shape, 0)
    lane = lax.broadcasted_iota(jnp.int32, shape, 1)

    def beside(field, at):
        down = jnp.where(row == extent_x - 1, below[at : at + 1, :], pltpu.roll(field, extent_x - 1, 0))
        up = jnp.where(row == 0, above[at : at + 1, :], pltpu.roll(field, 1, 0))
        right = jnp.where(lane == extent_y - 1, after[:, at : at + 1], pltpu.roll(field, extent_y - 1, 1))
        left = jnp.where(lane == 0, before[:, at : at + 1], pltpu.roll(field, 1, 1))
        return down, up, right, left

    cond = conduct[...]
    weights = [0.5 * (cond + other) for other in beside(cond, count_s)]
    for s in range(count_s):
        values = z[s]
        total = jnp.zeros(shape, F32)
        for weight, other in zip(weights, beside(values, s)):
            total = total + weight * (values - other)
        applied[s] = total
        curvature[s : s + 1, :] = jnp.broadcast_to(jnp.sum(values * total), (1, extent_y))
    leaf_map(applied, inverse, near, held)
    coeffs = rows_times(flat(applied), wide_high[...], wide_low[...], LANES)
    own[...] = coeffs
    send_chain(sent, coeffs, up_high, up_low)


def third_kernel(
    got, own, down_high, down_low, wide_high, wide_low, near, applied, sums, curvature, sent, mapped
):
    spread = tree(got, own, down_high, down_low)
    lanes = lax.broadcasted_iota(jnp.int32, (1, sent.shape[1]), 1)
    row = jnp.zeros((1, sent.shape[1]), F32)
    count_s = own.shape[0]
    for s in range(count_s):
        square = jnp.sum(near[s] * applied[s]) + jnp.sum(own[s : s + 1, :] * spread[s : s + 1, :])
        row = jnp.where(lanes == s, square, row)
        row = jnp.where(lanes == count_s + s, curvature[s : s + 1, :], row)
        row = jnp.where(lanes == 2 * count_s + s, sums[s : s + 1, :], row)
    sent[...] = jnp.broadcast_to(row, sent.shape)
    expand_into(mapped, spread, wide_high, wide_low, near)


def last_kernel(
    got, z, right, applied, mapped, solution_hbm, residual_hbm, direction_hbm, solution, residual, direction, sems
):
    count_s = z.shape[0]
    copies = [
        pltpu.make_async_copy(solution, solution_hbm, sems.at[0]),
        pltpu.make_async_copy(residual, residual_hbm, sems.at[1]),
        pltpu.make_async_copy(direction, direction_hbm, sems.at[2]),
    ]
    totals = jnp.sum(got[...], axis=0, keepdims=True)
    for s in range(count_s):
        curvature = totals[0:1, count_s + s : count_s + s + 1]
        step = totals[0:1, 2 * count_s + s : 2 * count_s + s + 1] / curvature
        ratio = step * totals[0:1, s : s + 1] / curvature - 1.0
        solution[s] = step * z[s]
        residual[s] = right[s] - step * applied[s]
        direction[s] = z[s] - step * mapped[s] + ratio * z[s]
    for copy in copies:
        copy.start()
    for copy in copies:
        copy.wait()


def leaf_map(values, inverse, out, held):
    count_s, extent_x, extent_y = values.shape
    blocks_x = extent_x // LBX
    rows = count_s * blocks_x
    group = lax.broadcasted_iota(jnp.int32, (rows, extent_y), 1) // LBY
    owner = lax.rem(lax.broadcasted_iota(jnp.int32, (rows, extent_y), 0), blocks_x)

    def regroup(lines):
        outs = []
        for q in range(len(lines)):
            out_q = lines[q]
            for a in range(len(lines)):
                if a != q:
                    turned = pltpu.roll(lines[a], ((a - q) * LBY) % extent_y, 1)
                    out_q = jnp.where(group == a, turned, out_q)
            outs.append(out_q)
        return outs

    lines = [
        jnp.concatenate(
            [values[s, p * LBX + a : p * LBX + a + 1, :] for s in range(count_s) for p in range(blocks_x)], axis=0
        )
        for a in range(LBX)
    ]
    mapped = []
    for q, block in enumerate(regroup(lines)):
        wide = jnp.concatenate([jnp.where(owner == p, block, 0.0) for p in range(blocks_x)], axis=1)
        stack = jnp.concatenate([inverse[p, q] for p in range(blocks_x)], axis=0)
        mapped.append(rows_times(wide, *parts(stack)))
    for a, line in enumerate(regroup(mapped)):
        held[a] = line
    for s in range(count_s):
        for p in range(blocks_x):
            for a in range(LBX):
                out[s, p * LBX + a : p * LBX + a + 1, :] = held[a, s * blocks_x + p : s * blocks_x + p + 1, :]


def pair_exchange(inner_value, outer_value, axis):
    count = lax.axis_size(axis)
    inner = [(i, i ^ 1) for i in range(count)]
    outer = []
    for i in range(1, count - 1, 2):
        outer += [(i, i + 1), (i + 1, i)]
    inner_value = lax.ppermute(inner_value, axis, inner)
    outer_value = lax.ppermute(outer_value, axis, outer)
    return inner_value, outer_value


def on_device(
    right_side,
    conductivity,
    leaf_inverse,
    front_basis,
    leaf_transfer,
    node_transfer,
    leaf_front,
    node_front,
):
    levels = node_front.shape[2]
    count = 1 << levels
    count_s, extent_x, extent_y = right_side.shape
    rank = front_basis.shape[-1]
    basis = front_basis.reshape(extent_x * extent_y, rank)
    leaf_t, node_t = leaf_transfer[0, 0], node_transfer[0, 0]
    leaf_f, node_f = leaf_front[0, 0], node_front[0, 0]
    field = (count_s, extent_x, extent_y)
    cells = extent_x * extent_y

    def pair(*shape):
        return (in_vmem(*shape, dtype=BF16),) * 2

    sent, own, wide_high, wide_low, up_high, up_low, moves, right_side, conductivity = call(
        project_kernel,
        (
            in_hbm(count, count_s, rank),
            in_vmem(count_s, rank),
            *pair(rank, cells),
            *pair(rank, levels * rank),
            in_vmem(levels, rank, rank),
            in_vmem(*field),
            in_vmem(extent_x, extent_y),
        ),
        (),
        10**6,
        (
            pltpu.VMEM((cells, rank), F32),
            pltpu.VMEM((count, count_s, rank), F32),
            pltpu.SemaphoreType.DMA((5 + PIECES,)),
        ),
        (leaf_t, node_t, right_side, basis, conductivity),
        written=1,
    )
    got = lax.all_to_all(sent, AXES, 0, 0)
    held = pltpu.VMEM((LBX, count_s * extent_x // LBX, extent_y), F32)
    near, down_high, down_low, inverse = call(
        window_kernel,
        (in_vmem(*field), *pair((levels + 1) * rank, rank), in_vmem(*leaf_inverse.shape)),
        (right_side, moves, up_high, up_low),
        10**7,
        (pltpu.VMEM((levels + 1, rank, rank), F32), held, pltpu.SemaphoreType.DMA((3,))),
        (leaf_f, node_f, leaf_inverse),
    )
    edge = (count_s + 1, extent_y)
    first_z, x_inner, x_outer, y_inner, y_outer, sums = call(
        first_kernel,
        [in_vmem(*s) for s in (field, edge, edge, (extent_x, extent_y), (extent_x, extent_y), (count_s, extent_y))],
        (got, own, down_high, down_low, wide_high, wide_low, near, right_side, conductivity),
        10**6,
    )
    x_inner, x_outer = pair_exchange(x_inner, x_outer, "gx")
    y_inner, y_outer = pair_exchange(y_inner, y_outer, "gy")
    applied, near, sent, own, curvature = call(
        second_kernel,
        (
            in_vmem(*field),
            in_vmem(*field),
            in_vmem(count, count_s, rank),
            in_vmem(count_s, rank),
            in_vmem(count_s, extent_y),
        ),
        (x_inner, x_outer, y_inner, y_outer, first_z, conductivity, wide_high, wide_low, up_high, up_low, inverse),
        10**6,
        (held,),
    )
    got = lax.all_to_all(sent, AXES, 0, 0)
    sent, mapped = call(
        third_kernel,
        (in_vmem(count, extent_y), in_vmem(*field)),
        (got, own, down_high, down_low, wide_high, wide_low, near, applied, sums, curvature),
        10**6,
    )
    got = lax.all_to_all(sent, AXES, 0, 0, tiled=True)
    return call(
        last_kernel,
        (in_hbm(*field),) * 3,
        (got, first_z, right_side, applied, mapped),
        10**6,
        (pltpu.VMEM(field, F32),) * 3 + (pltpu.SemaphoreType.DMA((3,)),),
        written=3,
    )


def solution(mesh):
    return jax.shard_map(
        on_device,
        mesh=mesh,
        in_specs=(
            P(None, "gx", "gy"),
            P("gx", "gy"),
            P("gx", "gy", None, None),
            P("gx", "gy", None),
            P("gx", "gy", None, None),
            P("gx", "gy", None, None, None),
            P("gx", "gy", None, None),
            P("gx", "gy", None, None, None),
        ),
        out_specs=(P(None, "gx", "gy"), P(None, "gx", "gy"), P(None, "gx", "gy")),
        check_vma=False,
    )
```

```python
import jax
import jax.numpy as jnp
from jax import lax
from jax.experimental import pallas as pl
from jax.experimental.pallas import tpu as pltpu
from jax.sharding import PartitionSpec as P

LBX = 4
LBY = 32
AXES = ("gx", "gy")
F32 = jnp.float32
BF16 = jnp.bfloat16
VMEM_LIMIT = 12 << 20
PIECES = 2


ROWS = (((1,), (0,)), ((), ()))
LANES = (((1,), (1,)), ((), ()))


def parts(value):
    high = value.astype(BF16)
    return high, (value - high.astype(F32)).astype(BF16)


def stacked(rows):
    high = rows.astype(BF16).astype(F32)
    rest = rows - high
    middle = rest.astype(BF16).astype(F32)
    return jnp.concatenate([high, middle, rest - middle], axis=0).astype(BF16)


def rows_times(rows, high, low, dims=ROWS):
    split = stacked(rows)
    count = rows.shape[0]
    total = lax.dot_general(split, low, dims, preferred_element_type=F32)
    total = total + lax.dot_general(split, high, dims, preferred_element_type=F32)
    return total[:count] + (total[count : 2 * count] + total[2 * count :])


def product(a, b):
    high, low = parts(b)
    left = jnp.concatenate(parts(a), axis=0)
    count = a.shape[0]
    total = lax.dot_general(left, low, ROWS, preferred_element_type=F32)
    total = total + lax.dot_general(left, high, ROWS, preferred_element_type=F32)
    return total[:count] + total[count:]


def in_vmem(*shape, dtype=F32):
    return pltpu.VMEM(shape, dtype)


def in_hbm(*shape, dtype=F32):
    return pltpu.HBM(shape, dtype)


def call(body, outs, arrays, flops, scratch=(), fetched=(), written=0):
    vmem = pl.BlockSpec(memory_space=pltpu.VMEM)
    hbm = pl.BlockSpec(memory_space=pltpu.HBM)
    size = sum(a.size * a.dtype.itemsize for a in arrays)
    fetched = [pltpu.with_memory_space_constraint(a, pltpu.HBM) for a in fetched]
    return pl.pallas_call(
        body,
        out_shape=tuple(outs),
        in_specs=[hbm] * len(fetched) + [vmem] * len(arrays),
        out_specs=(hbm,) * written + (vmem,) * (len(outs) - written),
        scratch_shapes=scratch,
        compiler_params=pltpu.CompilerParams(vmem_limit_bytes=VMEM_LIMIT),
        cost_estimate=pl.CostEstimate(flops=flops, bytes_accessed=size, transcendentals=0),
    )(*fetched, *arrays)


def place():
    return lax.axis_index("gx") * lax.axis_size("gy") + lax.axis_index("gy")


def at_end(axis):
    at = lax.axis_index(axis)
    return jnp.logical_or(at == 0, at == lax.axis_size(axis) - 1)


def odd(axis):
    return lax.rem(lax.axis_index(axis), 2) == 1


def cousins(me, level):
    return ((me >> (level - 1)) ^ 1) << (level - 1)


def flat(ref):
    return jnp.concatenate([ref[:, x, :] for x in range(ref.shape[1])], axis=1)


def send_rows(sent, chain):
    me = place()
    count_s = chain[0].shape[0]
    for level in range(1, len(chain) + 1):
        size = 1 << (level - 1)
        rows = jnp.broadcast_to(chain[level - 1][None], (size,) + chain[level - 1].shape)
        sent[pl.ds(cousins(me, level), size), 0:count_s, :] = rows
    sent[me, 0:count_s, :] = jnp.zeros(chain[0].shape, F32)


def project_kernel(
    leaf_t, node_t, values_hbm, basis_hbm, conduct_hbm,
    sent_hbm, own, wide_high, wide_low, up_high, up_low, moves, values, conduct, basis, sent, sems,
):
    levels, rank = moves.shape[0], moves.shape[1]
    piece = basis.shape[0] // PIECES
    slabs = [slice(i * piece, (i + 1) * piece) for i in range(PIECES)]
    pairs = [(leaf_t, moves.at[0]), (node_t, moves.at[pl.ds(1, levels - 1)]), (values_hbm, values)]
    pairs += [(basis_hbm.at[pl.ds(i * piece, piece)], basis.at[pl.ds(i * piece, piece)]) for i in range(PIECES)]
    pairs += [(conduct_hbm, conduct), (sent, sent_hbm)]
    copies = [pltpu.make_async_copy(source, target, sems.at[i]) for i, (source, target) in enumerate(pairs)]
    for copy in copies[:-1]:
        copy.start()
    copies[2].wait()
    rows = flat(values)
    coeffs = jnp.zeros(own.shape, F32)
    copies[0].wait()
    copies[1].wait()
    ups = [moves[0]]
    both = [product(moves[h], moves[h + 1]) for h in range(0, levels - 1, 2)]
    waiting = list(enumerate(slabs))
    while len(ups) < levels:
        h = len(ups) - 1
        if h % 2 == 0:
            ups.append(product(ups[h - 1], both[h // 2]) if h else both[0])
            if waiting:
                i, at = waiting.pop(0)
                copies[3 + i].wait()
                coeffs = coeffs + rows_times(rows[:, at], *parts(basis[at, :]))
        else:
            ups.append(product(ups[h], moves[h + 1]))
    for i, at in waiting:
        copies[3 + i].wait()
        coeffs = coeffs + rows_times(rows[:, at], *parts(basis[at, :]))
    for h in range(levels):
        at = slice(h * rank, (h + 1) * rank)
        up_high[:, at], up_low[:, at] = parts(ups[h])
    own[...] = coeffs
    send_chain(sent, coeffs, up_high, up_low)
    copies[-1].start()
    for at in slabs:
        wide_high[:, at], wide_low[:, at] = parts(basis[at, :].T)
    copies[-2].wait()
    copies[-1].wait()


def send_chain(sent, coeffs, up_high, up_low):
    rank = coeffs.shape[1]
    chain = rows_times(coeffs, up_high[...], up_low[...])
    send_rows(sent, [chain[:, i : i + rank] for i in range(0, chain.shape[1], rank)])


def window_kernel(
    leaf_f, node_f, inverse_hbm, values, moves, up_high, up_low,
    near, down_high, down_low, inverse, fronts, held, sems,
):
    levels, rank = moves.shape[0], moves.shape[1]
    copies = [
        pltpu.make_async_copy(leaf_f, fronts.at[0], sems.at[0]),
        pltpu.make_async_copy(node_f, fronts.at[pl.ds(1, levels)], sems.at[1]),
        pltpu.make_async_copy(inverse_hbm, inverse, sems.at[2]),
    ]
    for copy in copies:
        copy.start()
    columns = [slice(h * rank, (h + 1) * rank) for h in range(levels + 1)]
    back = [(up_high[:, at].astype(F32) + up_low[:, at].astype(F32)).T for at in columns[:levels]]
    copies[0].wait()
    copies[1].wait()
    total = [fronts[0]] + [product(fronts[h + 1], back[h]) for h in range(levels)]
    for h in range(levels, -1, -1):
        if h == levels // 2:
            copies[2].wait()
            leaf_map(values, inverse, near, held)
        if h < levels:
            total[h] = total[h] + product(moves[h], total[h + 1])
        down_high[columns[h], :], down_low[columns[h], :] = parts(total[h])


def tree(got, own, down_high, down_low):
    me = place()
    count_s, rank = own.shape
    rows = [own[...]]
    for level in range(1, down_high.shape[0] // rank):
        size = 1 << (level - 1)
        rows.append(jnp.sum(got[pl.ds(cousins(me, level), size), 0:count_s, :], axis=0))
    return rows_times(jnp.concatenate(rows, axis=1), down_high[...], down_low[...])


def expand_into(out, spread, wide_high, wide_low, near):
    far = rows_times(spread, wide_high[...], wide_low[...])
    width = out.shape[2]
    for x in range(out.shape[1]):
        out[:, x, :] = near[:, x, :] + far[:, x * width : (x + 1) * width]


def edge_column(values, conduct, at):
    lane = lax.broadcasted_iota(jnp.int32, conduct.shape, 1)
    column = jnp.broadcast_to(conduct[:, at : at + 1], conduct.shape)
    for s in range(values.shape[0]):
        column = jnp.where(lane == s, jnp.broadcast_to(values[s, :, at : at + 1], conduct.shape), column)
    return column


def first_kernel(
    got, own, down_high, down_low, wide_high, wide_low, near, right, conduct,
    z, x_inner, x_outer, y_inner, y_outer, sums,
):
    expand_into(z, tree(got, own, down_high, down_low), wide_high, wide_low, near)
    count_s, extent_x, extent_y = z.shape
    odd_x, odd_y = odd("gx"), odd("gy")
    for s in range(count_s):
        head, tail = z[s, 0:1, :], z[s, extent_x - 1 : extent_x, :]
        x_inner[s : s + 1, :] = jnp.where(odd_x, head, tail)
        x_outer[s : s + 1, :] = jnp.where(odd_x, tail, head)
    head, tail = conduct[0:1, :], conduct[extent_x - 1 : extent_x, :]
    x_inner[count_s : count_s + 1, :] = jnp.where(odd_x, head, tail)
    x_outer[count_s : count_s + 1, :] = jnp.where(odd_x, tail, head)
    values, cond = z[...], conduct[...]
    head, tail = edge_column(values, cond, 0), edge_column(values, cond, extent_y - 1)
    y_inner[...] = jnp.where(odd_y, head, tail)
    y_outer[...] = jnp.where(odd_y, tail, head)
    for s in range(count_s):
        sums[s : s + 1, :] = jnp.broadcast_to(jnp.sum(right[s] * values[s]), (1, extent_y))


def second_kernel(
    x_inner, x_outer, y_inner, y_outer, z, conduct, wide_high, wide_low, up_high, up_low, inverse,
    applied, near, sent, own, curvature, held,
):
    count_s, extent_x, extent_y = z.shape
    odd_x, odd_y = odd("gx"), odd("gy")
    x_far = jnp.where(at_end("gx"), 0.0, x_outer[...])
    y_far = jnp.where(at_end("gy"), 0.0, y_outer[...])
    above = jnp.where(odd_x, x_inner[...], x_far)
    below = jnp.where(odd_x, x_far, x_inner[...])
    before = jnp.where(odd_y, y_inner[...], y_far)
    after = jnp.where(odd_y, y_far, y_inner[...])
    shape = (extent_x, extent_y)
    row = lax.broadcasted_iota(jnp.int32, shape, 0)
    lane = lax.broadcasted_iota(jnp.int32, shape, 1)

    def beside(field, at):
        down = jnp.where(row == extent_x - 1, below[at : at + 1, :], pltpu.roll(field, extent_x - 1, 0))
        up = jnp.where(row == 0, above[at : at + 1, :], pltpu.roll(field, 1, 0))
        right = jnp.where(lane == extent_y - 1, after[:, at : at + 1], pltpu.roll(field, extent_y - 1, 1))
        left = jnp.where(lane == 0, before[:, at : at + 1], pltpu.roll(field, 1, 1))
        return down, up, right, left

    cond = conduct[...]
    weights = [0.5 * (cond + other) for other in beside(cond, count_s)]
    for s in range(count_s):
        values = z[s]
        total = jnp.zeros(shape, F32)
        for weight, other in zip(weights, beside(values, s)):
            total = total + weight * (values - other)
        applied[s] = total
        curvature[s : s + 1, :] = jnp.broadcast_to(jnp.sum(values * total), (1, extent_y))
    leaf_map(applied, inverse, near, held)
    coeffs = rows_times(flat(applied), wide_high[...], wide_low[...], LANES)
    own[...] = coeffs
    send_chain(sent, coeffs, up_high, up_low)


def third_kernel(
    got, own, down_high, down_low, wide_high, wide_low, near, applied, sums, curvature, sent, mapped
):
    spread = tree(got, own, down_high, down_low)
    lanes = lax.broadcasted_iota(jnp.int32, (1, sent.shape[1]), 1)
    row = jnp.zeros((1, sent.shape[1]), F32)
    count_s = own.shape[0]
    for s in range(count_s):
        square = jnp.sum(near[s] * applied[s]) + jnp.sum(own[s : s + 1, :] * spread[s : s + 1, :])
        row = jnp.where(lanes == s, square, row)
        row = jnp.where(lanes == count_s + s, curvature[s : s + 1, :], row)
        row = jnp.where(lanes == 2 * count_s + s, sums[s : s + 1, :], row)
    sent[...] = jnp.broadcast_to(row, sent.shape)
    expand_into(mapped, spread, wide_high, wide_low, near)


def last_kernel(
    got, z, right, applied, mapped, solution_hbm, residual_hbm, direction_hbm, solution, residual, direction, sems
):
    count_s = z.shape[0]
    copies = [
        pltpu.make_async_copy(solution, solution_hbm, sems.at[0]),
        pltpu.make_async_copy(residual, residual_hbm, sems.at[1]),
        pltpu.make_async_copy(direction, direction_hbm, sems.at[2]),
    ]
    totals = jnp.sum(got[...], axis=0, keepdims=True)
    for s in range(count_s):
        curvature = totals[0:1, count_s + s : count_s + s + 1]
        step = totals[0:1, 2 * count_s + s : 2 * count_s + s + 1] / curvature
        ratio = step * totals[0:1, s : s + 1] / curvature - 1.0
        solution[s] = step * z[s]
        residual[s] = right[s] - step * applied[s]
        direction[s] = z[s] - step * mapped[s] + ratio * z[s]
    for copy in copies:
        copy.start()
    for copy in copies:
        copy.wait()


def leaf_map(values, inverse, out, held):
    count_s, extent_x, extent_y = values.shape
    blocks_x = extent_x // LBX
    rows = count_s * blocks_x
    group = lax.broadcasted_iota(jnp.int32, (rows, extent_y), 1) // LBY
    owner = lax.rem(lax.broadcasted_iota(jnp.int32, (rows, extent_y), 0), blocks_x)

    def regroup(lines):
        outs = []
        for q in range(len(lines)):
            out_q = lines[q]
            for a in range(len(lines)):
                if a != q:
                    turned = pltpu.roll(lines[a], ((a - q) * LBY) % extent_y, 1)
                    out_q = jnp.where(group == a, turned, out_q)
            outs.append(out_q)
        return outs

    lines = [
        jnp.concatenate(
            [values[s, p * LBX + a : p * LBX + a + 1, :] for s in range(count_s) for p in range(blocks_x)], axis=0
        )
        for a in range(LBX)
    ]
    mapped = []
    for q, block in enumerate(regroup(lines)):
        wide = jnp.concatenate([jnp.where(owner == p, block, 0.0) for p in range(blocks_x)], axis=1)
        stack = jnp.concatenate([inverse[p, q] for p in range(blocks_x)], axis=0)
        mapped.append(rows_times(wide, *parts(stack)))
    for a, line in enumerate(regroup(mapped)):
        held[a] = line
    for s in range(count_s):
        for p in range(blocks_x):
            for a in range(LBX):
                out[s, p * LBX + a : p * LBX + a + 1, :] = held[a, s * blocks_x + p : s * blocks_x + p + 1, :]


def swap(value, pairs):
    return lax.ppermute(value, AXES, pairs + [(j, i) for i, j in pairs])


def matchings():
    wide, deep = lax.axis_size("gx"), lax.axis_size("gy")

    def along(first, second):
        return [
            ((i, j), (i + di, j + dj))
            for i in range(first[0], first[1], first[2])
            for j in range(second[0], second[1], second[2])
            for di, dj in [(first[3], second[3])]
        ]

    everywhere_x, everywhere_y = (0, wide, 1, 0), (0, deep, 1, 0)
    ends_x, ends_y = (0, wide, max(wide - 1, 1), 0), (0, deep, max(deep - 1, 1), 0)
    sets = {
        "gx_inner": along((0, wide - 1, 2, 1), everywhere_y),
        "gx_outer": along((1, wide - 1, 2, 1), everywhere_y) + along(ends_x, (0, deep - 1, 2, 1)),
        "gy_inner": along(everywhere_x, (0, deep - 1, 2, 1)),
        "gy_outer": along(everywhere_x, (1, deep - 1, 2, 1)) + along((0, wide - 1, 2, 1), ends_y),
    }
    return {name: [(i * deep + j, k * deep + l) for (i, j), (k, l) in pairs] for name, pairs in sets.items()}


def on_device(
    right_side,
    conductivity,
    leaf_inverse,
    front_basis,
    leaf_transfer,
    node_transfer,
    leaf_front,
    node_front,
):
    levels = node_front.shape[2]
    count = 1 << levels
    count_s, extent_x, extent_y = right_side.shape
    rank = front_basis.shape[-1]
    basis = front_basis.reshape(extent_x * extent_y, rank)
    leaf_t, node_t = leaf_transfer[0, 0], node_transfer[0, 0]
    leaf_f, node_f = leaf_front[0, 0], node_front[0, 0]
    field = (count_s, extent_x, extent_y)
    cells = extent_x * extent_y

    def pair(*shape):
        return (in_vmem(*shape, dtype=BF16),) * 2

    sent, own, wide_high, wide_low, up_high, up_low, moves, right_side, conductivity = call(
        project_kernel,
        (
            in_hbm(count, count_s, rank),
            in_vmem(count_s, rank),
            *pair(rank, cells),
            *pair(rank, levels * rank),
            in_vmem(levels, rank, rank),
            in_vmem(*field),
            in_vmem(extent_x, extent_y),
        ),
        (),
        10**6,
        (
            pltpu.VMEM((cells, rank), F32),
            pltpu.VMEM((count, count_s, rank), F32),
            pltpu.SemaphoreType.DMA((5 + PIECES,)),
        ),
        (leaf_t, node_t, right_side, basis, conductivity),
        written=1,
    )
    got = lax.all_to_all(sent, AXES, 0, 0)
    held = pltpu.VMEM((LBX, count_s * extent_x // LBX, extent_y), F32)
    near, down_high, down_low, inverse = call(
        window_kernel,
        (in_vmem(*field), *pair((levels + 1) * rank, rank), in_vmem(*leaf_inverse.shape)),
        (right_side, moves, up_high, up_low),
        10**7,
        (pltpu.VMEM((levels + 1, rank, rank), F32), held, pltpu.SemaphoreType.DMA((3,))),
        (leaf_f, node_f, leaf_inverse),
    )
    edge = (count_s + 1, extent_y)
    first_z, x_inner, x_outer, y_inner, y_outer, sums = call(
        first_kernel,
        [in_vmem(*s) for s in (field, edge, edge, (extent_x, extent_y), (extent_x, extent_y), (count_s, extent_y))],
        (got, own, down_high, down_low, wide_high, wide_low, near, right_side, conductivity),
        10**6,
    )
    pairs = matchings()
    x_inner, x_outer = swap(x_inner, pairs["gx_inner"]), swap(x_outer, pairs["gx_outer"])
    y_inner, y_outer = swap(y_inner, pairs["gy_inner"]), swap(y_outer, pairs["gy_outer"])
    applied, near, sent, own, curvature = call(
        second_kernel,
        (
            in_vmem(*field),
            in_vmem(*field),
            in_vmem(count, count_s, rank),
            in_vmem(count_s, rank),
            in_vmem(count_s, extent_y),
        ),
        (x_inner, x_outer, y_inner, y_outer, first_z, conductivity, wide_high, wide_low, up_high, up_low, inverse),
        10**6,
        (held,),
    )
    got = lax.all_to_all(sent, AXES, 0, 0)
    sent, mapped = call(
        third_kernel,
        (in_vmem(count, extent_y), in_vmem(*field)),
        (got, own, down_high, down_low, wide_high, wide_low, near, applied, sums, curvature),
        10**6,
    )
    got = lax.all_to_all(sent, AXES, 0, 0, tiled=True)
    return call(
        last_kernel,
        (in_hbm(*field),) * 3,
        (got, first_z, right_side, applied, mapped),
        10**6,
        (pltpu.VMEM(field, F32),) * 3 + (pltpu.SemaphoreType.DMA((3,)),),
        written=3,
    )


def solution(mesh):
    return jax.shard_map(
        on_device,
        mesh=mesh,
        in_specs=(
            P(None, "gx", "gy"),
            P("gx", "gy"),
            P("gx", "gy", None, None),
            P("gx", "gy", None),
            P("gx", "gy", None, None),
            P("gx", "gy", None, None, None),
            P("gx", "gy", None, None),
            P("gx", "gy", None, None, None),
        ),
        out_specs=(P(None, "gx", "gy"), P(None, "gx", "gy"), P(None, "gx", "gy")),
        check_vma=False,
    )
```

```python
import jax
import jax.numpy as jnp
from jax import lax
from jax.experimental import pallas as pl
from jax.experimental.pallas import tpu as pltpu
from jax.sharding import PartitionSpec as P

LBX = 4
LBY = 32
AXES = ("gx", "gy")
F32 = jnp.float32
BF16 = jnp.bfloat16
VMEM_LIMIT = 12 << 20
PIECES = 2


ROWS = (((1,), (0,)), ((), ()))
LANES = (((1,), (1,)), ((), ()))


def parts(value):
    high = value.astype(BF16)
    return high, (value - high.astype(F32)).astype(BF16)


def stacked(rows):
    high = rows.astype(BF16).astype(F32)
    rest = rows - high
    middle = rest.astype(BF16).astype(F32)
    return jnp.concatenate([high, middle, rest - middle], axis=0).astype(BF16)


def rows_times(rows, high, low, dims=ROWS):
    split = stacked(rows)
    count = rows.shape[0]
    total = lax.dot_general(split, low, dims, preferred_element_type=F32)
    total = total + lax.dot_general(split, high, dims, preferred_element_type=F32)
    return total[:count] + (total[count : 2 * count] + total[2 * count :])


def product(a, b):
    high, low = parts(b)
    left = jnp.concatenate(parts(a), axis=0)
    count = a.shape[0]
    total = lax.dot_general(left, low, ROWS, preferred_element_type=F32)
    total = total + lax.dot_general(left, high, ROWS, preferred_element_type=F32)
    return total[:count] + total[count:]


def in_vmem(*shape, dtype=F32):
    return pltpu.VMEM(shape, dtype)


def in_hbm(*shape, dtype=F32):
    return pltpu.HBM(shape, dtype)


def call(body, outs, arrays, flops, scratch=(), fetched=(), written=0):
    vmem = pl.BlockSpec(memory_space=pltpu.VMEM)
    hbm = pl.BlockSpec(memory_space=pltpu.HBM)
    size = sum(a.size * a.dtype.itemsize for a in arrays)
    fetched = [pltpu.with_memory_space_constraint(a, pltpu.HBM) for a in fetched]
    return pl.pallas_call(
        body,
        out_shape=tuple(outs),
        in_specs=[hbm] * len(fetched) + [vmem] * len(arrays),
        out_specs=(hbm,) * written + (vmem,) * (len(outs) - written),
        scratch_shapes=scratch,
        compiler_params=pltpu.CompilerParams(vmem_limit_bytes=VMEM_LIMIT),
        cost_estimate=pl.CostEstimate(flops=flops, bytes_accessed=size, transcendentals=0),
    )(*fetched, *arrays)


def place():
    return lax.axis_index("gx") * lax.axis_size("gy") + lax.axis_index("gy")


def at_end(axis):
    at = lax.axis_index(axis)
    return jnp.logical_or(at == 0, at == lax.axis_size(axis) - 1)


def odd(axis):
    return lax.rem(lax.axis_index(axis), 2) == 1


def cousins(me, level):
    return ((me >> (level - 1)) ^ 1) << (level - 1)


def flat(ref):
    return jnp.concatenate([ref[:, x, :] for x in range(ref.shape[1])], axis=1)


def send_rows(sent, chain):
    me = place()
    count_s = chain[0].shape[0]
    for level in range(1, len(chain) + 1):
        size = 1 << (level - 1)
        rows = jnp.broadcast_to(chain[level - 1][None], (size,) + chain[level - 1].shape)
        sent[pl.ds(cousins(me, level), size), 0:count_s, :] = rows
    sent[me, 0:count_s, :] = jnp.zeros(chain[0].shape, F32)


def project_kernel(
    leaf_t, node_t, values_hbm, basis_hbm, conduct_hbm,
    sent_hbm, own, wide_high, wide_low, up_high, up_low, moves, values, conduct, basis, sent, sems,
):
    levels, rank = moves.shape[0], moves.shape[1]
    piece = basis.shape[0] // PIECES
    slabs = [slice(i * piece, (i + 1) * piece) for i in range(PIECES)]
    pairs = [(leaf_t, moves.at[0]), (node_t, moves.at[pl.ds(1, levels - 1)]), (values_hbm, values)]
    pairs += [(basis_hbm.at[pl.ds(i * piece, piece)], basis.at[pl.ds(i * piece, piece)]) for i in range(PIECES)]
    pairs += [(conduct_hbm, conduct), (sent, sent_hbm)]
    copies = [pltpu.make_async_copy(source, target, sems.at[i]) for i, (source, target) in enumerate(pairs)]
    for copy in copies[:-1]:
        copy.start()
    copies[2].wait()
    rows = flat(values)
    coeffs = jnp.zeros(own.shape, F32)
    copies[0].wait()
    copies[1].wait()
    ups = [moves[0]]
    both = [product(moves[h], moves[h + 1]) for h in range(0, levels - 1, 2)]
    waiting = list(enumerate(slabs))
    while len(ups) < levels:
        h = len(ups) - 1
        if h % 2 == 0:
            ups.append(product(ups[h - 1], both[h // 2]) if h else both[0])
            if waiting:
                i, at = waiting.pop(0)
                copies[3 + i].wait()
                coeffs = coeffs + rows_times(rows[:, at], *parts(basis[at, :]))
        else:
            ups.append(product(ups[h], moves[h + 1]))
    for i, at in waiting:
        copies[3 + i].wait()
        coeffs = coeffs + rows_times(rows[:, at], *parts(basis[at, :]))
    for h in range(levels):
        at = slice(h * rank, (h + 1) * rank)
        up_high[:, at], up_low[:, at] = parts(ups[h])
    own[...] = coeffs
    send_chain(sent, coeffs, up_high, up_low)
    copies[-1].start()
    for at in slabs:
        wide_high[:, at], wide_low[:, at] = parts(basis[at, :].T)
    copies[-2].wait()
    copies[-1].wait()


def send_chain(sent, coeffs, up_high, up_low):
    rank = coeffs.shape[1]
    chain = rows_times(coeffs, up_high[...], up_low[...])
    send_rows(sent, [chain[:, i : i + rank] for i in range(0, chain.shape[1], rank)])


def window_kernel(
    leaf_f, node_f, inverse_hbm, values, moves, up_high, up_low,
    near, down_high, down_low, meet_high, meet_low, inverse, fronts, held, sems,
):
    levels, rank = moves.shape[0], moves.shape[1]
    copies = [
        pltpu.make_async_copy(leaf_f, fronts.at[0], sems.at[0]),
        pltpu.make_async_copy(node_f, fronts.at[pl.ds(1, levels)], sems.at[1]),
        pltpu.make_async_copy(inverse_hbm, inverse, sems.at[2]),
    ]
    for copy in copies:
        copy.start()
    columns = [slice(h * rank, (h + 1) * rank) for h in range(levels + 1)]
    back = [(up_high[:, at].astype(F32) + up_low[:, at].astype(F32)).T for at in columns[:levels]]
    copies[0].wait()
    copies[1].wait()
    total = [fronts[0]] + [product(fronts[h + 1], back[h]) for h in range(levels)]
    for h in range(levels, -1, -1):
        if h == levels // 2:
            copies[2].wait()
            leaf_map(values, inverse, near, held)
        if h < levels:
            total[h] = total[h] + product(moves[h], total[h + 1])
        down_high[columns[h], :], down_low[columns[h], :] = parts(total[h])
        if h > 0:
            second = lax.rem(place() >> (h - 1), 2) == 1
            at = columns[h - 1]
            plain = up_high[:, at].astype(F32) + up_low[:, at].astype(F32)
            meet_high[:, at], meet_low[:, at] = parts(jnp.where(second, total[h].T, plain))


def tree(got, own, down_high, down_low):
    me = place()
    count_s, rank = own.shape
    rows = [own[...]]
    for level in range(1, down_high.shape[0] // rank):
        size = 1 << (level - 1)
        rows.append(jnp.sum(got[pl.ds(cousins(me, level), size), 0:count_s, :], axis=0))
    return rows_times(jnp.concatenate(rows, axis=1), down_high[...], down_low[...])


def expand_into(out, spread, wide_high, wide_low, near):
    far = rows_times(spread, wide_high[...], wide_low[...])
    width = out.shape[2]
    for x in range(out.shape[1]):
        out[:, x, :] = near[:, x, :] + far[:, x * width : (x + 1) * width]


def edge_column(values, conduct, at):
    lane = lax.broadcasted_iota(jnp.int32, conduct.shape, 1)
    column = jnp.broadcast_to(conduct[:, at : at + 1], conduct.shape)
    for s in range(values.shape[0]):
        column = jnp.where(lane == s, jnp.broadcast_to(values[s, :, at : at + 1], conduct.shape), column)
    return column


def first_kernel(
    got, own, down_high, down_low, wide_high, wide_low, near, right, conduct,
    z, x_inner, x_outer, y_inner, y_outer, sums,
):
    expand_into(z, tree(got, own, down_high, down_low), wide_high, wide_low, near)
    count_s, extent_x, extent_y = z.shape
    odd_x, odd_y = odd("gx"), odd("gy")
    for s in range(count_s):
        head, tail = z[s, 0:1, :], z[s, extent_x - 1 : extent_x, :]
        x_inner[s : s + 1, :] = jnp.where(odd_x, head, tail)
        x_outer[s : s + 1, :] = jnp.where(odd_x, tail, head)
    head, tail = conduct[0:1, :], conduct[extent_x - 1 : extent_x, :]
    x_inner[count_s : count_s + 1, :] = jnp.where(odd_x, head, tail)
    x_outer[count_s : count_s + 1, :] = jnp.where(odd_x, tail, head)
    values, cond = z[...], conduct[...]
    head, tail = edge_column(values, cond, 0), edge_column(values, cond, extent_y - 1)
    y_inner[...] = jnp.where(odd_y, head, tail)
    y_outer[...] = jnp.where(odd_y, tail, head)
    for s in range(count_s):
        sums[s : s + 1, :] = jnp.broadcast_to(jnp.sum(right[s] * values[s]), (1, extent_y))


def second_kernel(
    x_inner, x_outer, y_inner, y_outer, z, conduct, wide_high, wide_low, meet_high, meet_low, down_high, down_low, inverse,
    sums, applied, near, sent, home, held,
):
    count_s, extent_x, extent_y = z.shape
    odd_x, odd_y = odd("gx"), odd("gy")
    x_far = jnp.where(at_end("gx"), 0.0, x_outer[...])
    y_far = jnp.where(at_end("gy"), 0.0, y_outer[...])
    above = jnp.where(odd_x, x_inner[...], x_far)
    below = jnp.where(odd_x, x_far, x_inner[...])
    before = jnp.where(odd_y, y_inner[...], y_far)
    after = jnp.where(odd_y, y_far, y_inner[...])
    shape = (extent_x, extent_y)
    row = lax.broadcasted_iota(jnp.int32, shape, 0)
    lane = lax.broadcasted_iota(jnp.int32, shape, 1)

    def beside(field, at):
        down = jnp.where(row == extent_x - 1, below[at : at + 1, :], pltpu.roll(field, extent_x - 1, 0))
        up = jnp.where(row == 0, above[at : at + 1, :], pltpu.roll(field, 1, 0))
        right = jnp.where(lane == extent_y - 1, after[:, at : at + 1], pltpu.roll(field, extent_y - 1, 1))
        left = jnp.where(lane == 0, before[:, at : at + 1], pltpu.roll(field, 1, 1))
        return down, up, right, left

    cond = conduct[...]
    weights = [0.5 * (cond + other) for other in beside(cond, count_s)]
    lanes = lax.broadcasted_iota(jnp.int32, (1, extent_y), 1)
    curvature = []
    for s in range(count_s):
        values = z[s]
        total = jnp.zeros(shape, F32)
        for weight, other in zip(weights, beside(values, s)):
            total = total + weight * (values - other)
        applied[s] = total
        curvature.append(jnp.sum(values * total))
    coeffs = rows_times(flat(applied), wide_high[...], wide_low[...], LANES)
    leaf_map(applied, inverse, near, held)
    rank = coeffs.shape[1]
    chain = rows_times(coeffs, meet_high[...], meet_low[...])
    back = rows_times(coeffs, down_high[0:rank, :], down_low[0:rank, :])
    home[...] = back
    levels = chain.shape[1] // rank
    for level in range(levels):
        row = chain[:, level * rank : (level + 1) * rank]
        sent[:, level] = jnp.broadcast_to(row[None], (sent.shape[0],) + row.shape)
    packed = []
    for s in range(count_s):
        square = jnp.sum(near[s] * applied[s]) + jnp.sum(coeffs[s : s + 1, :] * back[s : s + 1, :])
        row = jnp.where(lanes == 0, square, jnp.where(lanes == 1, curvature[s], 0.0))
        packed.append(jnp.where(lanes == 2, sums[s : s + 1, :], row))
    row = jnp.concatenate(packed, axis=0)
    sent[:, levels] = jnp.broadcast_to(row[None], (sent.shape[0],) + row.shape)


def last_kernel(
    got, home, meet_high, meet_low, wide_high, wide_low, near, z, right, applied,
    solution_hbm, residual_hbm, direction_hbm, solution, residual, direction, mapped, sems,
):
    me = place()
    levels, count_s = got.shape[1] - 1, got.shape[2]
    copies = [
        pltpu.make_async_copy(solution, solution_hbm, sems.at[0]),
        pltpu.make_async_copy(residual, residual_hbm, sems.at[1]),
        pltpu.make_async_copy(direction, direction_hbm, sems.at[2]),
    ]
    heard, cross = [], jnp.zeros(home.shape, F32)
    for level in range(1, levels + 1):
        size = 1 << (level - 1)
        heard.append(jnp.sum(got[pl.ds(cousins(me, level), size), level - 1], axis=0))
        rows = got[:, level - 1]
        for _ in range(level - 1):
            rows = rows.reshape((rows.shape[0] // 2, 2) + rows.shape[1:])
            rows = rows[:, 0] + rows[:, 1]
        rows = rows.reshape((rows.shape[0] // 2, 2) + rows.shape[1:])
        cross = cross + jnp.sum(rows[:, 0] * rows[:, 1], axis=0)
    totals = jnp.sum(got[:, levels], axis=0)
    square = totals[:, 0:1] + 2.0 * jnp.sum(cross, axis=1, keepdims=True)
    curvature = totals[:, 1:2]
    steps = totals[:, 2:3] / curvature
    ratios = steps * square / curvature - 1.0
    for s in range(count_s):
        solution[s] = steps[s : s + 1] * z[s]
        residual[s] = right[s] - steps[s : s + 1] * applied[s]
    copies[0].start()
    copies[1].start()
    spread = home[...] + rows_times(jnp.concatenate(heard, axis=1), meet_high[...], meet_low[...], LANES)
    expand_into(mapped, spread, wide_high, wide_low, near)
    for s in range(count_s):
        direction[s] = z[s] - steps[s : s + 1] * mapped[s] + ratios[s : s + 1] * z[s]
    copies[2].start()
    for copy in copies:
        copy.wait()


def leaf_map(values, inverse, out, held):
    count_s, extent_x, extent_y = values.shape
    blocks_x = extent_x // LBX
    rows = count_s * blocks_x
    group = lax.broadcasted_iota(jnp.int32, (rows, extent_y), 1) // LBY
    owner = lax.rem(lax.broadcasted_iota(jnp.int32, (rows, extent_y), 0), blocks_x)

    def regroup(lines):
        outs = []
        for q in range(len(lines)):
            out_q = lines[q]
            for a in range(len(lines)):
                if a != q:
                    turned = pltpu.roll(lines[a], ((a - q) * LBY) % extent_y, 1)
                    out_q = jnp.where(group == a, turned, out_q)
            outs.append(out_q)
        return outs

    lines = [
        jnp.concatenate(
            [values[s, p * LBX + a : p * LBX + a + 1, :] for s in range(count_s) for p in range(blocks_x)], axis=0
        )
        for a in range(LBX)
    ]
    mapped = []
    for q, block in enumerate(regroup(lines)):
        wide = jnp.concatenate([jnp.where(owner == p, block, 0.0) for p in range(blocks_x)], axis=1)
        stack = jnp.concatenate([inverse[p, q] for p in range(blocks_x)], axis=0)
        mapped.append(rows_times(wide, *parts(stack)))
    for a, line in enumerate(regroup(mapped)):
        held[a] = line
    for s in range(count_s):
        for p in range(blocks_x):
            for a in range(LBX):
                out[s, p * LBX + a : p * LBX + a + 1, :] = held[a, s * blocks_x + p : s * blocks_x + p + 1, :]


def swap(value, pairs):
    return lax.ppermute(value, AXES, pairs + [(j, i) for i, j in pairs])


def matchings():
    wide, deep = lax.axis_size("gx"), lax.axis_size("gy")

    def along(first, second):
        return [
            ((i, j), (i + di, j + dj))
            for i in range(first[0], first[1], first[2])
            for j in range(second[0], second[1], second[2])
            for di, dj in [(first[3], second[3])]
        ]

    everywhere_x, everywhere_y = (0, wide, 1, 0), (0, deep, 1, 0)
    ends_x, ends_y = (0, wide, max(wide - 1, 1), 0), (0, deep, max(deep - 1, 1), 0)
    sets = {
        "gx_inner": along((0, wide - 1, 2, 1), everywhere_y),
        "gx_outer": along((1, wide - 1, 2, 1), everywhere_y) + along(ends_x, (0, deep - 1, 2, 1)),
        "gy_inner": along(everywhere_x, (0, deep - 1, 2, 1)),
        "gy_outer": along(everywhere_x, (1, deep - 1, 2, 1)) + along((0, wide - 1, 2, 1), ends_y),
    }
    return {name: [(i * deep + j, k * deep + l) for (i, j), (k, l) in pairs] for name, pairs in sets.items()}


def on_device(
    right_side,
    conductivity,
    leaf_inverse,
    front_basis,
    leaf_transfer,
    node_transfer,
    leaf_front,
    node_front,
):
    levels = node_front.shape[2]
    count = 1 << levels
    count_s, extent_x, extent_y = right_side.shape
    rank = front_basis.shape[-1]
    basis = front_basis.reshape(extent_x * extent_y, rank)
    leaf_t, node_t = leaf_transfer[0, 0], node_transfer[0, 0]
    leaf_f, node_f = leaf_front[0, 0], node_front[0, 0]
    field = (count_s, extent_x, extent_y)
    cells = extent_x * extent_y

    def pair(*shape):
        return (in_vmem(*shape, dtype=BF16),) * 2

    sent, own, wide_high, wide_low, up_high, up_low, moves, right_side, conductivity = call(
        project_kernel,
        (
            in_hbm(count, count_s, rank),
            in_vmem(count_s, rank),
            *pair(rank, cells),
            *pair(rank, levels * rank),
            in_vmem(levels, rank, rank),
            in_vmem(*field),
            in_vmem(extent_x, extent_y),
        ),
        (),
        10**6,
        (
            pltpu.VMEM((cells, rank), F32),
            pltpu.VMEM((count, count_s, rank), F32),
            pltpu.SemaphoreType.DMA((5 + PIECES,)),
        ),
        (leaf_t, node_t, right_side, basis, conductivity),
        written=1,
    )
    got = lax.all_to_all(sent, AXES, 0, 0)
    held = pltpu.VMEM((LBX, count_s * extent_x // LBX, extent_y), F32)
    near, down_high, down_low, meet_high, meet_low, inverse = call(
        window_kernel,
        (
            in_vmem(*field),
            *pair((levels + 1) * rank, rank),
            *pair(rank, levels * rank),
            in_vmem(*leaf_inverse.shape),
        ),
        (right_side, moves, up_high, up_low),
        10**7,
        (pltpu.VMEM((levels + 1, rank, rank), F32), held, pltpu.SemaphoreType.DMA((3,))),
        (leaf_f, node_f, leaf_inverse),
    )
    edge = (count_s + 1, extent_y)
    first_z, x_inner, x_outer, y_inner, y_outer, sums = call(
        first_kernel,
        [in_vmem(*s) for s in (field, edge, edge, (extent_x, extent_y), (extent_x, extent_y), (count_s, extent_y))],
        (got, own, down_high, down_low, wide_high, wide_low, near, right_side, conductivity),
        10**6,
    )
    pairs = matchings()
    x_inner, x_outer = swap(x_inner, pairs["gx_inner"]), swap(x_outer, pairs["gx_outer"])
    y_inner, y_outer = swap(y_inner, pairs["gy_inner"]), swap(y_outer, pairs["gy_outer"])
    applied, near, sent, home = call(
        second_kernel,
        (
            in_vmem(*field),
            in_vmem(*field),
            in_vmem(count, levels + 1, count_s, rank),
            in_vmem(count_s, rank),
        ),
        (
            x_inner, x_outer, y_inner, y_outer, first_z, conductivity,
            wide_high, wide_low, meet_high, meet_low, down_high, down_low, inverse, sums,
        ),
        10**6,
        (held,),
    )
    got = lax.all_to_all(sent, AXES, 0, 0)
    return call(
        last_kernel,
        (in_hbm(*field),) * 3,
        (got, home, meet_high, meet_low, wide_high, wide_low, near, first_z, right_side, applied),
        10**6,
        (pltpu.VMEM(field, F32),) * 4 + (pltpu.SemaphoreType.DMA((3,)),),
        written=3,
    )


def solution(mesh):
    return jax.shard_map(
        on_device,
        mesh=mesh,
        in_specs=(
            P(None, "gx", "gy"),
            P("gx", "gy"),
            P("gx", "gy", None, None),
            P("gx", "gy", None),
            P("gx", "gy", None, None),
            P("gx", "gy", None, None, None),
            P("gx", "gy", None, None),
            P("gx", "gy", None, None, None),
        ),
        out_specs=(P(None, "gx", "gy"), P(None, "gx", "gy"), P(None, "gx", "gy")),
        check_vma=False,
    )
```

```python
import jax
import jax.numpy as jnp
from jax import lax
from jax.experimental import pallas as pl
from jax.experimental.pallas import tpu as pltpu
from jax.sharding import PartitionSpec as P

LBX = 4
LBY = 32
AXES = ("gx", "gy")
F32 = jnp.float32
BF16 = jnp.bfloat16
VMEM_LIMIT = 12 << 20
PIECES = 2


ROWS = (((1,), (0,)), ((), ()))
LANES = (((1,), (1,)), ((), ()))


def parts(value):
    high = value.astype(BF16)
    return high, (value - high.astype(F32)).astype(BF16)


def stacked(rows):
    high = rows.astype(BF16).astype(F32)
    rest = rows - high
    middle = rest.astype(BF16).astype(F32)
    return jnp.concatenate([high, middle, rest - middle], axis=0).astype(BF16)


def rows_times(rows, high, low, dims=ROWS):
    split = stacked(rows)
    count = rows.shape[0]
    total = lax.dot_general(split, low, dims, preferred_element_type=F32)
    total = total + lax.dot_general(split, high, dims, preferred_element_type=F32)
    return total[:count] + (total[count : 2 * count] + total[2 * count :])


def product(a, b):
    high, low = parts(b)
    left = jnp.concatenate(parts(a), axis=0)
    count = a.shape[0]
    total = lax.dot_general(left, low, ROWS, preferred_element_type=F32)
    total = total + lax.dot_general(left, high, ROWS, preferred_element_type=F32)
    return total[:count] + total[count:]


def in_vmem(*shape, dtype=F32):
    return pltpu.VMEM(shape, dtype)


def in_hbm(*shape, dtype=F32):
    return pltpu.HBM(shape, dtype)


def call(body, outs, arrays, flops, scratch=(), fetched=(), written=0):
    vmem = pl.BlockSpec(memory_space=pltpu.VMEM)
    hbm = pl.BlockSpec(memory_space=pltpu.HBM)
    size = sum(a.size * a.dtype.itemsize for a in arrays)
    fetched = [pltpu.with_memory_space_constraint(a, pltpu.HBM) for a in fetched]
    return pl.pallas_call(
        body,
        out_shape=tuple(outs),
        in_specs=[hbm] * len(fetched) + [vmem] * len(arrays),
        out_specs=(hbm,) * written + (vmem,) * (len(outs) - written),
        scratch_shapes=scratch,
        compiler_params=pltpu.CompilerParams(vmem_limit_bytes=VMEM_LIMIT),
        cost_estimate=pl.CostEstimate(flops=flops, bytes_accessed=size, transcendentals=0),
    )(*fetched, *arrays)


def place():
    return lax.axis_index("gx") * lax.axis_size("gy") + lax.axis_index("gy")


def at_end(axis):
    at = lax.axis_index(axis)
    return jnp.logical_or(at == 0, at == lax.axis_size(axis) - 1)


def odd(axis):
    return lax.rem(lax.axis_index(axis), 2) == 1


def cousins(me, level):
    return ((me >> (level - 1)) ^ 1) << (level - 1)


def flat(ref):
    return jnp.concatenate([ref[:, x, :] for x in range(ref.shape[1])], axis=1)


def send_rows(sent, chain):
    me = place()
    count_s = chain[0].shape[0]
    for level in range(1, len(chain) + 1):
        size = 1 << (level - 1)
        rows = jnp.broadcast_to(chain[level - 1][None], (size,) + chain[level - 1].shape)
        sent[pl.ds(cousins(me, level), size), 0:count_s, :] = rows
    sent[me, 0:count_s, :] = jnp.zeros(chain[0].shape, F32)


def project_kernel(
    leaf_t, node_t, values_hbm, basis_hbm, conduct_hbm,
    sent_hbm, own, wide_high, wide_low, up_high, up_low, values, conduct, moves, basis, sent, sems,
):
    levels, rank = moves.shape[0], moves.shape[1]
    piece = basis.shape[0] // PIECES
    slabs = [slice(i * piece, (i + 1) * piece) for i in range(PIECES)]
    pairs = [(leaf_t, moves.at[0]), (node_t, moves.at[pl.ds(1, levels - 1)]), (values_hbm, values)]
    pairs += [(basis_hbm.at[pl.ds(i * piece, piece)], basis.at[pl.ds(i * piece, piece)]) for i in range(PIECES)]
    pairs += [(conduct_hbm, conduct), (sent, sent_hbm)]
    copies = [pltpu.make_async_copy(source, target, sems.at[i]) for i, (source, target) in enumerate(pairs)]
    for copy in copies[:-1]:
        copy.start()
    copies[2].wait()
    rows = flat(values)
    coeffs = jnp.zeros(own.shape, F32)
    copies[0].wait()
    copies[1].wait()
    ups = [moves[0]]
    both = [product(moves[h], moves[h + 1]) for h in range(0, levels - 1, 2)]
    waiting = list(enumerate(slabs))
    while len(ups) < levels:
        h = len(ups) - 1
        if h % 2 == 0:
            ups.append(product(ups[h - 1], both[h // 2]) if h else both[0])
            if waiting:
                i, at = waiting.pop(0)
                copies[3 + i].wait()
                coeffs = coeffs + rows_times(rows[:, at], *parts(basis[at, :]))
        else:
            ups.append(product(ups[h], moves[h + 1]))
    for i, at in waiting:
        copies[3 + i].wait()
        coeffs = coeffs + rows_times(rows[:, at], *parts(basis[at, :]))
    for h in range(levels):
        at = slice(h * rank, (h + 1) * rank)
        up_high[:, at], up_low[:, at] = parts(ups[h])
    own[...] = coeffs
    send_chain(sent, coeffs, up_high, up_low)
    copies[-1].start()
    for at in slabs:
        wide_high[:, at], wide_low[:, at] = parts(basis[at, :].T)
    copies[-2].wait()
    copies[-1].wait()


def send_chain(sent, coeffs, up_high, up_low):
    rank = coeffs.shape[1]
    chain = rows_times(coeffs, up_high[...], up_low[...])
    send_rows(sent, [chain[:, i : i + rank] for i in range(0, chain.shape[1], rank)])


def window_kernel(
    leaf_f, node_f, inverse_hbm, leaf_t, node_t, values, up_high, up_low,
    near, down_high, down_low, meet_high, meet_low, inverse, moves, fronts, held, sems,
):
    levels, rank = moves.shape[0], moves.shape[1]
    copies = [
        pltpu.make_async_copy(leaf_f, fronts.at[0], sems.at[0]),
        pltpu.make_async_copy(node_f, fronts.at[pl.ds(1, levels)], sems.at[1]),
        pltpu.make_async_copy(inverse_hbm, inverse, sems.at[2]),
        pltpu.make_async_copy(leaf_t, moves.at[0], sems.at[3]),
        pltpu.make_async_copy(node_t, moves.at[pl.ds(1, moves.shape[0] - 1)], sems.at[4]),
    ]
    for i in (0, 1, 3, 4, 2):
        copies[i].start()
    columns = [slice(h * rank, (h + 1) * rank) for h in range(levels + 1)]
    back = [(up_high[:, at].astype(F32) + up_low[:, at].astype(F32)).T for at in columns[:levels]]
    for i in (0, 1, 3, 4):
        copies[i].wait()
    total = [fronts[0]] + [product(fronts[h + 1], back[h]) for h in range(levels)]
    for h in range(levels, -1, -1):
        if h == levels // 2:
            copies[2].wait()
            leaf_map(values, inverse, near, held)
        if h < levels:
            total[h] = total[h] + product(moves[h], total[h + 1])
        down_high[columns[h], :], down_low[columns[h], :] = parts(total[h])
        if h > 0:
            second = lax.rem(place() >> (h - 1), 2) == 1
            at = columns[h - 1]
            plain = up_high[:, at].astype(F32) + up_low[:, at].astype(F32)
            meet_high[:, at], meet_low[:, at] = parts(jnp.where(second, total[h].T, plain))
        else:
            meet_high[:, columns[levels]], meet_low[:, columns[levels]] = parts(total[0])


def tree(got, own, down_high, down_low):
    me = place()
    count_s, rank = own.shape
    rows = [own[...]]
    for level in range(1, down_high.shape[0] // rank):
        size = 1 << (level - 1)
        rows.append(jnp.sum(got[pl.ds(cousins(me, level), size), 0:count_s, :], axis=0))
    return rows_times(jnp.concatenate(rows, axis=1), down_high[...], down_low[...])


def expand_into(out, spread, wide_high, wide_low, near):
    far = rows_times(spread, wide_high[...], wide_low[...])
    width = out.shape[2]
    for x in range(out.shape[1]):
        out[:, x, :] = near[:, x, :] + far[:, x * width : (x + 1) * width]


def edge_column(values, conduct, at):
    lane = lax.broadcasted_iota(jnp.int32, conduct.shape, 1)
    column = jnp.broadcast_to(conduct[:, at : at + 1], conduct.shape)
    for s in range(values.shape[0]):
        column = jnp.where(lane == s, jnp.broadcast_to(values[s, :, at : at + 1], conduct.shape), column)
    return column


def first_kernel(
    got, own, down_high, down_low, wide_high, wide_low, near, right, conduct,
    z, x_inner, x_outer, y_inner, y_outer, sums,
):
    expand_into(z, tree(got, own, down_high, down_low), wide_high, wide_low, near)
    count_s, extent_x, extent_y = z.shape
    odd_x, odd_y = odd("gx"), odd("gy")
    for s in range(count_s):
        head, tail = z[s, 0:1, :], z[s, extent_x - 1 : extent_x, :]
        x_inner[s : s + 1, :] = jnp.where(odd_x, head, tail)
        x_outer[s : s + 1, :] = jnp.where(odd_x, tail, head)
    head, tail = conduct[0:1, :], conduct[extent_x - 1 : extent_x, :]
    x_inner[count_s : count_s + 1, :] = jnp.where(odd_x, head, tail)
    x_outer[count_s : count_s + 1, :] = jnp.where(odd_x, tail, head)
    values, cond = z[...], conduct[...]
    head, tail = edge_column(values, cond, 0), edge_column(values, cond, extent_y - 1)
    y_inner[...] = jnp.where(odd_y, head, tail)
    y_outer[...] = jnp.where(odd_y, tail, head)
    for s in range(count_s):
        sums[s : s + 1, :] = jnp.broadcast_to(jnp.sum(right[s] * values[s]), (1, extent_y))


def second_kernel(
    x_inner, x_outer, y_inner, y_outer, z, conduct, wide_high, wide_low, meet_high, meet_low, inverse,
    sums, applied, near, sent, home, held,
):
    count_s, extent_x, extent_y = z.shape
    odd_x, odd_y = odd("gx"), odd("gy")
    x_far = jnp.where(at_end("gx"), 0.0, x_outer[...])
    y_far = jnp.where(at_end("gy"), 0.0, y_outer[...])
    above = jnp.where(odd_x, x_inner[...], x_far)
    below = jnp.where(odd_x, x_far, x_inner[...])
    before = jnp.where(odd_y, y_inner[...], y_far)
    after = jnp.where(odd_y, y_far, y_inner[...])
    shape = (extent_x, extent_y)
    row = lax.broadcasted_iota(jnp.int32, shape, 0)
    lane = lax.broadcasted_iota(jnp.int32, shape, 1)

    def beside(field, at):
        down = jnp.where(row == extent_x - 1, below[at : at + 1, :], pltpu.roll(field, extent_x - 1, 0))
        up = jnp.where(row == 0, above[at : at + 1, :], pltpu.roll(field, 1, 0))
        right = jnp.where(lane == extent_y - 1, after[:, at : at + 1], pltpu.roll(field, extent_y - 1, 1))
        left = jnp.where(lane == 0, before[:, at : at + 1], pltpu.roll(field, 1, 1))
        return down, up, right, left

    cond = conduct[...]
    weights = [0.5 * (cond + other) for other in beside(cond, count_s)]
    lanes = lax.broadcasted_iota(jnp.int32, (1, extent_y), 1)
    curvature = []
    for s in range(count_s):
        values = z[s]
        total = jnp.zeros(shape, F32)
        for weight, other in zip(weights, beside(values, s)):
            total = total + weight * (values - other)
        applied[s] = total
        curvature.append(jnp.sum(values * total))
    coeffs = rows_times(flat(applied), wide_high[...], wide_low[...], LANES)
    leaf_map(applied, inverse, near, held)
    rank = coeffs.shape[1]
    chain = rows_times(coeffs, meet_high[...], meet_low[...])
    levels = chain.shape[1] // rank - 1
    back = chain[:, levels * rank :]
    home[...] = back
    for level in range(levels):
        row = chain[:, level * rank : (level + 1) * rank]
        sent[:, level] = jnp.broadcast_to(row[None], (sent.shape[0],) + row.shape)
    packed = []
    for s in range(count_s):
        square = jnp.sum(near[s] * applied[s]) + jnp.sum(coeffs[s : s + 1, :] * back[s : s + 1, :])
        row = jnp.where(lanes == 0, square, jnp.where(lanes == 1, curvature[s], 0.0))
        packed.append(jnp.where(lanes == 2, sums[s : s + 1, :], row))
    row = jnp.concatenate(packed, axis=0)
    sent[:, levels] = jnp.broadcast_to(row[None], (sent.shape[0],) + row.shape)


def last_kernel(
    got, home, meet_high, meet_low, wide_high, wide_low, near, z, right, applied,
    solution_hbm, residual_hbm, direction_hbm, solution, residual, direction, mapped, sems,
):
    me = place()
    levels, count_s = got.shape[1] - 1, got.shape[2]
    copies = [
        pltpu.make_async_copy(solution, solution_hbm, sems.at[0]),
        pltpu.make_async_copy(residual, residual_hbm, sems.at[1]),
        pltpu.make_async_copy(direction, direction_hbm, sems.at[2]),
    ]
    heard, cross = [], jnp.zeros(home.shape, F32)
    for level in range(1, levels + 1):
        size = 1 << (level - 1)
        heard.append(jnp.sum(got[pl.ds(cousins(me, level), size), level - 1], axis=0))
        rows = got[:, level - 1]
        for _ in range(level - 1):
            rows = rows.reshape((rows.shape[0] // 2, 2) + rows.shape[1:])
            rows = rows[:, 0] + rows[:, 1]
        rows = rows.reshape((rows.shape[0] // 2, 2) + rows.shape[1:])
        cross = cross + jnp.sum(rows[:, 0] * rows[:, 1], axis=0)
    totals = jnp.sum(got[:, levels], axis=0)
    square = totals[:, 0:1] + 2.0 * jnp.sum(cross, axis=1, keepdims=True)
    curvature = totals[:, 1:2]
    steps = totals[:, 2:3] / curvature
    ratios = steps * square / curvature - 1.0
    for s in range(count_s):
        solution[s] = steps[s : s + 1] * z[s]
        residual[s] = right[s] - steps[s : s + 1] * applied[s]
    copies[0].start()
    copies[1].start()
    rows = jnp.concatenate(heard, axis=1)
    spread = home[...] + rows_times(rows, meet_high[:, : rows.shape[1]], meet_low[:, : rows.shape[1]], LANES)
    expand_into(mapped, spread, wide_high, wide_low, near)
    for s in range(count_s):
        direction[s] = z[s] - steps[s : s + 1] * mapped[s] + ratios[s : s + 1] * z[s]
    copies[2].start()
    for copy in copies:
        copy.wait()


def leaf_map(values, inverse, out, held):
    count_s, extent_x, extent_y = values.shape
    blocks_x = extent_x // LBX
    rows = count_s * blocks_x
    group = lax.broadcasted_iota(jnp.int32, (rows, extent_y), 1) // LBY
    owner = lax.rem(lax.broadcasted_iota(jnp.int32, (rows, extent_y), 0), blocks_x)

    def regroup(lines):
        outs = []
        for q in range(len(lines)):
            out_q = lines[q]
            for a in range(len(lines)):
                if a != q:
                    turned = pltpu.roll(lines[a], ((a - q) * LBY) % extent_y, 1)
                    out_q = jnp.where(group == a, turned, out_q)
            outs.append(out_q)
        return outs

    lines = [
        jnp.concatenate(
            [values[s, p * LBX + a : p * LBX + a + 1, :] for s in range(count_s) for p in range(blocks_x)], axis=0
        )
        for a in range(LBX)
    ]
    mapped = []
    for q, block in enumerate(regroup(lines)):
        wide = jnp.concatenate([jnp.where(owner == p, block, 0.0) for p in range(blocks_x)], axis=1)
        stack = jnp.concatenate([inverse[p, q] for p in range(blocks_x)], axis=0)
        mapped.append(rows_times(wide, *parts(stack)))
    for a, line in enumerate(regroup(mapped)):
        held[a] = line
    for s in range(count_s):
        for p in range(blocks_x):
            for a in range(LBX):
                out[s, p * LBX + a : p * LBX + a + 1, :] = held[a, s * blocks_x + p : s * blocks_x + p + 1, :]


def swap(value, pairs):
    return lax.ppermute(value, AXES, pairs + [(j, i) for i, j in pairs])


def matchings():
    wide, deep = lax.axis_size("gx"), lax.axis_size("gy")

    def along(first, second):
        return [
            ((i, j), (i + di, j + dj))
            for i in range(first[0], first[1], first[2])
            for j in range(second[0], second[1], second[2])
            for di, dj in [(first[3], second[3])]
        ]

    everywhere_x, everywhere_y = (0, wide, 1, 0), (0, deep, 1, 0)
    ends_x, ends_y = (0, wide, max(wide - 1, 1), 0), (0, deep, max(deep - 1, 1), 0)
    sets = {
        "gx_inner": along((0, wide - 1, 2, 1), everywhere_y),
        "gx_outer": along((1, wide - 1, 2, 1), everywhere_y) + along(ends_x, (0, deep - 1, 2, 1)),
        "gy_inner": along(everywhere_x, (0, deep - 1, 2, 1)),
        "gy_outer": along(everywhere_x, (1, deep - 1, 2, 1)) + along((0, wide - 1, 2, 1), ends_y),
    }
    return {name: [(i * deep + j, k * deep + l) for (i, j), (k, l) in pairs] for name, pairs in sets.items()}


def on_device(
    right_side,
    conductivity,
    leaf_inverse,
    front_basis,
    leaf_transfer,
    node_transfer,
    leaf_front,
    node_front,
):
    levels = node_front.shape[2]
    count = 1 << levels
    count_s, extent_x, extent_y = right_side.shape
    rank = front_basis.shape[-1]
    basis = front_basis.reshape(extent_x * extent_y, rank)
    leaf_t, node_t = leaf_transfer[0, 0], node_transfer[0, 0]
    leaf_f, node_f = leaf_front[0, 0], node_front[0, 0]
    field = (count_s, extent_x, extent_y)
    cells = extent_x * extent_y

    def pair(*shape):
        return (in_vmem(*shape, dtype=BF16),) * 2

    sent, own, wide_high, wide_low, up_high, up_low, right_side, conductivity = call(
        project_kernel,
        (
            in_hbm(count, count_s, rank),
            in_vmem(count_s, rank),
            *pair(rank, cells),
            *pair(rank, levels * rank),
            in_vmem(*field),
            in_vmem(extent_x, extent_y),
        ),
        (),
        10**6,
        (
            pltpu.VMEM((levels, rank, rank), F32),
            pltpu.VMEM((cells, rank), F32),
            pltpu.VMEM((count, count_s, rank), F32),
            pltpu.SemaphoreType.DMA((5 + PIECES,)),
        ),
        (leaf_t, node_t, right_side, basis, conductivity),
        written=1,
    )
    got = lax.all_to_all(sent, AXES, 0, 0)
    held = pltpu.VMEM((LBX, count_s * extent_x // LBX, extent_y), F32)
    near, down_high, down_low, meet_high, meet_low, inverse = call(
        window_kernel,
        (
            in_vmem(*field),
            *pair((levels + 1) * rank, rank),
            *pair(rank, (levels + 1) * rank),
            in_vmem(*leaf_inverse.shape),
        ),
        (right_side, up_high, up_low),
        10**7,
        (
            pltpu.VMEM((levels, rank, rank), F32),
            pltpu.VMEM((levels + 1, rank, rank), F32),
            held,
            pltpu.SemaphoreType.DMA((5,)),
        ),
        (leaf_f, node_f, leaf_inverse, leaf_t, node_t),
    )
    edge = (count_s + 1, extent_y)
    first_z, x_inner, x_outer, y_inner, y_outer, sums = call(
        first_kernel,
        [in_vmem(*s) for s in (field, edge, edge, (extent_x, extent_y), (extent_x, extent_y), (count_s, extent_y))],
        (got, own, down_high, down_low, wide_high, wide_low, near, right_side, conductivity),
        10**6,
    )
    pairs = matchings()
    x_inner, x_outer = swap(x_inner, pairs["gx_inner"]), swap(x_outer, pairs["gx_outer"])
    y_inner, y_outer = swap(y_inner, pairs["gy_inner"]), swap(y_outer, pairs["gy_outer"])
    applied, near, sent, home = call(
        second_kernel,
        (
            in_vmem(*field),
            in_vmem(*field),
            in_vmem(count, levels + 1, count_s, rank),
            in_vmem(count_s, rank),
        ),
        (
            x_inner, x_outer, y_inner, y_outer, first_z, conductivity,
            wide_high, wide_low, meet_high, meet_low, inverse, sums,
        ),
        10**6,
        (held,),
    )
    got = lax.all_to_all(sent, AXES, 0, 0)
    return call(
        last_kernel,
        (in_hbm(*field),) * 3,
        (got, home, meet_high, meet_low, wide_high, wide_low, near, first_z, right_side, applied),
        10**6,
        (pltpu.VMEM(field, F32),) * 4 + (pltpu.SemaphoreType.DMA((3,)),),
        written=3,
    )


def solution(mesh):
    return jax.shard_map(
        on_device,
        mesh=mesh,
        in_specs=(
            P(None, "gx", "gy"),
            P("gx", "gy"),
            P("gx", "gy", None, None),
            P("gx", "gy", None),
            P("gx", "gy", None, None),
            P("gx", "gy", None, None, None),
            P("gx", "gy", None, None),
            P("gx", "gy", None, None, None),
        ),
        out_specs=(P(None, "gx", "gy"), P(None, "gx", "gy"), P(None, "gx", "gy")),
        check_vma=False,
    )
```

```python
import jax
import jax.numpy as jnp
from jax import lax
from jax.experimental import pallas as pl
from jax.experimental.pallas import tpu as pltpu
from jax.sharding import PartitionSpec as P

LBX = 4
LBY = 32
AXES = ("gx", "gy")
F32 = jnp.float32
BF16 = jnp.bfloat16
VMEM_LIMIT = 12 << 20
PIECES = 2


ROWS = (((1,), (0,)), ((), ()))
LANES = (((1,), (1,)), ((), ()))


def parts(value):
    high = value.astype(BF16)
    return high, (value - high.astype(F32)).astype(BF16)


def stacked(rows):
    high = rows.astype(BF16).astype(F32)
    rest = rows - high
    middle = rest.astype(BF16).astype(F32)
    return jnp.concatenate([high, middle, rest - middle], axis=0).astype(BF16)


def rows_times(rows, high, low, dims=ROWS):
    split = stacked(rows)
    count = rows.shape[0]
    total = lax.dot_general(split, low, dims, preferred_element_type=F32)
    total = total + lax.dot_general(split, high, dims, preferred_element_type=F32)
    return total[:count] + (total[count : 2 * count] + total[2 * count :])


def product(a, b):
    high, low = parts(b)
    left = jnp.concatenate(parts(a), axis=0)
    count = a.shape[0]
    total = lax.dot_general(left, low, ROWS, preferred_element_type=F32)
    total = total + lax.dot_general(left, high, ROWS, preferred_element_type=F32)
    return total[:count] + total[count:]


def in_vmem(*shape, dtype=F32):
    return pltpu.VMEM(shape, dtype)


def in_hbm(*shape, dtype=F32):
    return pltpu.HBM(shape, dtype)


def call(body, outs, arrays, flops, scratch=(), fetched=(), written=0):
    vmem = pl.BlockSpec(memory_space=pltpu.VMEM)
    hbm = pl.BlockSpec(memory_space=pltpu.HBM)
    size = sum(a.size * a.dtype.itemsize for a in arrays)
    fetched = [pltpu.with_memory_space_constraint(a, pltpu.HBM) for a in fetched]
    return pl.pallas_call(
        body,
        out_shape=tuple(outs),
        in_specs=[hbm] * len(fetched) + [vmem] * len(arrays),
        out_specs=(hbm,) * written + (vmem,) * (len(outs) - written),
        scratch_shapes=scratch,
        compiler_params=pltpu.CompilerParams(vmem_limit_bytes=VMEM_LIMIT),
        cost_estimate=pl.CostEstimate(flops=flops, bytes_accessed=size, transcendentals=0),
    )(*fetched, *arrays)


def place():
    return lax.axis_index("gx") * lax.axis_size("gy") + lax.axis_index("gy")


def at_end(axis):
    at = lax.axis_index(axis)
    return jnp.logical_or(at == 0, at == lax.axis_size(axis) - 1)


def odd(axis):
    return lax.rem(lax.axis_index(axis), 2) == 1


def cousins(me, level):
    return ((me >> (level - 1)) ^ 1) << (level - 1)


def flat(ref):
    return jnp.concatenate([ref[:, x, :] for x in range(ref.shape[1])], axis=1)


def send_rows(sent, chain):
    me = place()
    count_s = chain[0].shape[0]
    for level in range(1, len(chain) + 1):
        size = 1 << (level - 1)
        rows = jnp.broadcast_to(chain[level - 1][None], (size,) + chain[level - 1].shape)
        sent[pl.ds(cousins(me, level), size), 0:count_s, :] = rows
    sent[me, 0:count_s, :] = jnp.zeros(chain[0].shape, F32)


def project_kernel(
    leaf_t, node_t, values_hbm, basis_hbm, conduct_hbm,
    sent_hbm, own, wide_high, wide_low, up_high, up_low, values, conduct, moves, basis, sent, sems,
):
    levels, rank = moves.shape[0], moves.shape[1]
    piece = basis.shape[0] // PIECES
    slabs = [slice(i * piece, (i + 1) * piece) for i in range(PIECES)]
    pairs = [(leaf_t, moves.at[0]), (node_t, moves.at[pl.ds(1, levels - 1)]), (values_hbm, values)]
    pairs += [(basis_hbm.at[pl.ds(i * piece, piece)], basis.at[pl.ds(i * piece, piece)]) for i in range(PIECES)]
    pairs += [(conduct_hbm, conduct), (sent, sent_hbm)]
    copies = [pltpu.make_async_copy(source, target, sems.at[i]) for i, (source, target) in enumerate(pairs)]
    for copy in copies[:-1]:
        copy.start()
    copies[2].wait()
    rows = flat(values)
    coeffs = jnp.zeros(own.shape, F32)
    copies[0].wait()
    copies[1].wait()
    ups = [moves[0]]
    both = [product(moves[h], moves[h + 1]) for h in range(0, levels - 1, 2)]
    waiting = list(enumerate(slabs))
    while len(ups) < levels:
        h = len(ups) - 1
        if h % 2 == 0:
            ups.append(product(ups[h - 1], both[h // 2]) if h else both[0])
            if waiting:
                i, at = waiting.pop(0)
                copies[3 + i].wait()
                coeffs = coeffs + rows_times(rows[:, at], *parts(basis[at, :]))
        else:
            ups.append(product(ups[h], moves[h + 1]))
    for i, at in waiting:
        copies[3 + i].wait()
        coeffs = coeffs + rows_times(rows[:, at], *parts(basis[at, :]))
    for h in range(levels):
        at = slice(h * rank, (h + 1) * rank)
        up_high[:, at], up_low[:, at] = parts(ups[h])
    own[...] = coeffs
    send_chain(sent, coeffs, up_high, up_low)
    copies[-1].start()
    for at in slabs:
        wide_high[:, at], wide_low[:, at] = parts(basis[at, :].T)
    copies[-2].wait()
    copies[-1].wait()


def send_chain(sent, coeffs, up_high, up_low):
    rank = coeffs.shape[1]
    chain = rows_times(coeffs, up_high[...], up_low[...])
    send_rows(sent, [chain[:, i : i + rank] for i in range(0, chain.shape[1], rank)])


def window_kernel(
    leaf_f, node_f, inverse_hbm, leaf_t, node_t, values, up_high, up_low,
    near, down_high, down_low, meet_high, meet_low, inverse, moves, fronts, held, sems,
):
    levels, rank = moves.shape[0], moves.shape[1]
    copies = [
        pltpu.make_async_copy(leaf_f, fronts.at[0], sems.at[0]),
        pltpu.make_async_copy(node_f, fronts.at[pl.ds(1, levels)], sems.at[1]),
        pltpu.make_async_copy(inverse_hbm, inverse, sems.at[2]),
        pltpu.make_async_copy(leaf_t, moves.at[0], sems.at[3]),
        pltpu.make_async_copy(node_t, moves.at[pl.ds(1, moves.shape[0] - 1)], sems.at[4]),
    ]
    for i in (0, 1, 3, 4, 2):
        copies[i].start()
    columns = [slice(h * rank, (h + 1) * rank) for h in range(levels + 1)]
    back = [(up_high[:, at].astype(F32) + up_low[:, at].astype(F32)).T for at in columns[:levels]]
    for i in (0, 1, 3, 4):
        copies[i].wait()
    total = [fronts[0]] + [product(fronts[h + 1], back[h]) for h in range(levels)]
    for h in range(levels, -1, -1):
        if h == levels // 2:
            copies[2].wait()
            leaf_map(values, inverse, near, held)
        if h < levels:
            total[h] = total[h] + product(moves[h], total[h + 1])
        down_high[columns[h], :], down_low[columns[h], :] = parts(total[h])
        if h > 0:
            second = lax.rem(place() >> (h - 1), 2) == 1
            at = columns[h - 1]
            plain = up_high[:, at].astype(F32) + up_low[:, at].astype(F32)
            meet_high[:, at], meet_low[:, at] = parts(jnp.where(second, total[h].T, plain))
        else:
            meet_high[:, columns[levels]], meet_low[:, columns[levels]] = parts(total[0])


def tree(got, own, down_high, down_low):
    me = place()
    count_s, rank = own.shape
    rows = [own[...]]
    for level in range(1, down_high.shape[0] // rank):
        size = 1 << (level - 1)
        rows.append(jnp.sum(got[pl.ds(cousins(me, level), size), 0:count_s, :], axis=0))
    return rows_times(jnp.concatenate(rows, axis=1), down_high[...], down_low[...])


def expand_into(out, spread, wide_high, wide_low, near):
    far = rows_times(spread, wide_high[...], wide_low[...])
    width = out.shape[2]
    for x in range(out.shape[1]):
        out[:, x, :] = near[:, x, :] + far[:, x * width : (x + 1) * width]


def edge_column(values, conduct, at):
    lane = lax.broadcasted_iota(jnp.int32, conduct.shape, 1)
    column = jnp.broadcast_to(conduct[:, at : at + 1], conduct.shape)
    for s in range(values.shape[0]):
        column = jnp.where(lane == s, jnp.broadcast_to(values[s, :, at : at + 1], conduct.shape), column)
    return column


def first_kernel(
    got, own, down_high, down_low, wide_high, wide_low, near, right, conduct,
    z, x_inner, x_outer, y_inner, y_outer, sums,
):
    expand_into(z, tree(got, own, down_high, down_low), wide_high, wide_low, near)
    count_s, extent_x, extent_y = z.shape
    odd_x, odd_y = odd("gx"), odd("gy")
    for s in range(count_s):
        head, tail = z[s, 0:1, :], z[s, extent_x - 1 : extent_x, :]
        x_inner[s : s + 1, :] = jnp.where(odd_x, head, tail)
        x_outer[s : s + 1, :] = jnp.where(odd_x, tail, head)
    head, tail = conduct[0:1, :], conduct[extent_x - 1 : extent_x, :]
    x_inner[count_s : count_s + 1, :] = jnp.where(odd_x, head, tail)
    x_outer[count_s : count_s + 1, :] = jnp.where(odd_x, tail, head)
    values, cond = z[...], conduct[...]
    head, tail = edge_column(values, cond, 0), edge_column(values, cond, extent_y - 1)
    y_inner[...] = jnp.where(odd_y, head, tail)
    y_outer[...] = jnp.where(odd_y, tail, head)
    for s in range(count_s):
        sums[s : s + 1, :] = jnp.broadcast_to(jnp.sum(right[s] * values[s]), (1, extent_y))


def second_kernel(
    x_inner, x_outer, y_inner, y_outer, z, conduct, wide_high, wide_low, meet_high, meet_low, inverse,
    sums, applied, near, sent, home, held,
):
    count_s, extent_x, extent_y = z.shape
    odd_x, odd_y = odd("gx"), odd("gy")
    x_far = jnp.where(at_end("gx"), 0.0, x_outer[...])
    y_far = jnp.where(at_end("gy"), 0.0, y_outer[...])
    above = jnp.where(odd_x, x_inner[...], x_far)
    below = jnp.where(odd_x, x_far, x_inner[...])
    before = jnp.where(odd_y, y_inner[...], y_far)
    after = jnp.where(odd_y, y_far, y_inner[...])
    shape = (extent_x, extent_y)
    row = lax.broadcasted_iota(jnp.int32, shape, 0)
    lane = lax.broadcasted_iota(jnp.int32, shape, 1)

    def beside(field, at):
        down = jnp.where(row == extent_x - 1, below[at : at + 1, :], pltpu.roll(field, extent_x - 1, 0))
        up = jnp.where(row == 0, above[at : at + 1, :], pltpu.roll(field, 1, 0))
        right = jnp.where(lane == extent_y - 1, after[:, at : at + 1], pltpu.roll(field, extent_y - 1, 1))
        left = jnp.where(lane == 0, before[:, at : at + 1], pltpu.roll(field, 1, 1))
        return down, up, right, left

    cond = conduct[...]
    weights = [0.5 * (cond + other) for other in beside(cond, count_s)]
    lanes = lax.broadcasted_iota(jnp.int32, (1, extent_y), 1)
    curvature = []
    for s in range(count_s):
        values = z[s]
        total = jnp.zeros(shape, F32)
        for weight, other in zip(weights, beside(values, s)):
            total = total + weight * (values - other)
        applied[s] = total
        curvature.append(jnp.sum(values * total))
    coeffs = rows_times(flat(applied), wide_high[...], wide_low[...], LANES)
    leaf_map(applied, inverse, near, held)
    rank = coeffs.shape[1]
    chain = rows_times(coeffs, meet_high[...], meet_low[...])
    levels = chain.shape[1] // rank - 1
    back = chain[:, levels * rank :]
    home[...] = back
    for level in range(levels):
        row = chain[:, level * rank : (level + 1) * rank]
        sent[:, level] = jnp.broadcast_to(row[None], (sent.shape[0],) + row.shape)
    packed = []
    for s in range(count_s):
        square = jnp.sum(near[s] * applied[s]) + jnp.sum(coeffs[s : s + 1, :] * back[s : s + 1, :])
        row = jnp.where(lanes == 0, square, jnp.where(lanes == 1, curvature[s], 0.0))
        packed.append(jnp.where(lanes == 2, sums[s : s + 1, :], row))
    row = jnp.concatenate(packed, axis=0)
    sent[:, levels] = jnp.broadcast_to(row[None], (sent.shape[0],) + row.shape)


def last_kernel(
    got, home, meet_high, meet_low, wide_high, wide_low, near, z, right, applied,
    solution_hbm, residual_hbm, direction_hbm, solution, residual, direction, mapped, sems,
):
    me = place()
    levels, count_s = got.shape[1] - 1, got.shape[2]
    copies = [
        pltpu.make_async_copy(solution, solution_hbm, sems.at[0]),
        pltpu.make_async_copy(residual, residual_hbm, sems.at[1]),
    ]
    for part in range(2):
        at = pl.ds(part * (direction.shape[1] // 2), direction.shape[1] // 2)
        copies.append(pltpu.make_async_copy(direction.at[:, at], direction_hbm.at[:, at], sems.at[2 + part]))
    heard, cross = [], jnp.zeros(home.shape, F32)
    for level in range(1, levels + 1):
        size = 1 << (level - 1)
        heard.append(jnp.sum(got[pl.ds(cousins(me, level), size), level - 1], axis=0))
        rows = got[:, level - 1]
        for _ in range(level - 1):
            rows = rows.reshape((rows.shape[0] // 2, 2) + rows.shape[1:])
            rows = rows[:, 0] + rows[:, 1]
        rows = rows.reshape((rows.shape[0] // 2, 2) + rows.shape[1:])
        cross = cross + jnp.sum(rows[:, 0] * rows[:, 1], axis=0)
    totals = jnp.sum(got[:, levels], axis=0)
    square = totals[:, 0:1] + 2.0 * jnp.sum(cross, axis=1, keepdims=True)
    curvature = totals[:, 1:2]
    steps = totals[:, 2:3] / curvature
    ratios = steps * square / curvature - 1.0
    for s in range(count_s):
        solution[s] = steps[s : s + 1] * z[s]
        residual[s] = right[s] - steps[s : s + 1] * applied[s]
    copies[0].start()
    copies[1].start()
    rows = jnp.concatenate(heard, axis=1)
    spread = home[...] + rows_times(rows, meet_high[:, : rows.shape[1]], meet_low[:, : rows.shape[1]], LANES)
    extent_x, width = direction.shape[1], direction.shape[2]
    half = extent_x // 2
    for part in range(2):
        rows = slice(part * half, (part + 1) * half)
        cells = slice(part * half * width, (part + 1) * half * width)
        far = rows_times(spread, wide_high[:, cells], wide_low[:, cells])
        for x in range(half):
            at = part * half + x
            mapped[:, at, :] = near[:, at, :] + far[:, x * width : (x + 1) * width]
        for s in range(count_s):
            rest = z[s, rows, :] - steps[s : s + 1] * mapped[s, rows, :]
            direction[s, rows, :] = rest + ratios[s : s + 1] * z[s, rows, :]
        copies[2 + part].start()
    for copy in copies:
        copy.wait()


def leaf_map(values, inverse, out, held):
    count_s, extent_x, extent_y = values.shape
    blocks_x = extent_x // LBX
    rows = count_s * blocks_x
    group = lax.broadcasted_iota(jnp.int32, (rows, extent_y), 1) // LBY
    owner = lax.rem(lax.broadcasted_iota(jnp.int32, (rows, extent_y), 0), blocks_x)

    def regroup(lines):
        outs = []
        for q in range(len(lines)):
            out_q = lines[q]
            for a in range(len(lines)):
                if a != q:
                    turned = pltpu.roll(lines[a], ((a - q) * LBY) % extent_y, 1)
                    out_q = jnp.where(group == a, turned, out_q)
            outs.append(out_q)
        return outs

    lines = [
        jnp.concatenate(
            [values[s, p * LBX + a : p * LBX + a + 1, :] for s in range(count_s) for p in range(blocks_x)], axis=0
        )
        for a in range(LBX)
    ]
    mapped = []
    for q, block in enumerate(regroup(lines)):
        wide = jnp.concatenate([jnp.where(owner == p, block, 0.0) for p in range(blocks_x)], axis=1)
        stack = jnp.concatenate([inverse[p, q] for p in range(blocks_x)], axis=0)
        mapped.append(rows_times(wide, *parts(stack)))
    for a, line in enumerate(regroup(mapped)):
        held[a] = line
    for s in range(count_s):
        for p in range(blocks_x):
            for a in range(LBX):
                out[s, p * LBX + a : p * LBX + a + 1, :] = held[a, s * blocks_x + p : s * blocks_x + p + 1, :]


def swap(value, pairs):
    return lax.ppermute(value, AXES, pairs + [(j, i) for i, j in pairs])


def matchings():
    wide, deep = lax.axis_size("gx"), lax.axis_size("gy")

    def along(first, second):
        return [
            ((i, j), (i + di, j + dj))
            for i in range(first[0], first[1], first[2])
            for j in range(second[0], second[1], second[2])
            for di, dj in [(first[3], second[3])]
        ]

    everywhere_x, everywhere_y = (0, wide, 1, 0), (0, deep, 1, 0)
    ends_x, ends_y = (0, wide, max(wide - 1, 1), 0), (0, deep, max(deep - 1, 1), 0)
    sets = {
        "gx_inner": along((0, wide - 1, 2, 1), everywhere_y),
        "gx_outer": along((1, wide - 1, 2, 1), everywhere_y) + along(ends_x, (0, deep - 1, 2, 1)),
        "gy_inner": along(everywhere_x, (0, deep - 1, 2, 1)),
        "gy_outer": along(everywhere_x, (1, deep - 1, 2, 1)) + along((0, wide - 1, 2, 1), ends_y),
    }
    return {name: [(i * deep + j, k * deep + l) for (i, j), (k, l) in pairs] for name, pairs in sets.items()}


def on_device(
    right_side,
    conductivity,
    leaf_inverse,
    front_basis,
    leaf_transfer,
    node_transfer,
    leaf_front,
    node_front,
):
    levels = node_front.shape[2]
    count = 1 << levels
    count_s, extent_x, extent_y = right_side.shape
    rank = front_basis.shape[-1]
    basis = front_basis.reshape(extent_x * extent_y, rank)
    leaf_t, node_t = leaf_transfer[0, 0], node_transfer[0, 0]
    leaf_f, node_f = leaf_front[0, 0], node_front[0, 0]
    field = (count_s, extent_x, extent_y)
    cells = extent_x * extent_y

    def pair(*shape):
        return (in_vmem(*shape, dtype=BF16),) * 2

    sent, own, wide_high, wide_low, up_high, up_low, right_side, conductivity = call(
        project_kernel,
        (
            in_hbm(count, count_s, rank),
            in_vmem(count_s, rank),
            *pair(rank, cells),
            *pair(rank, levels * rank),
            in_vmem(*field),
            in_vmem(extent_x, extent_y),
        ),
        (),
        10**6,
        (
            pltpu.VMEM((levels, rank, rank), F32),
            pltpu.VMEM((cells, rank), F32),
            pltpu.VMEM((count, count_s, rank), F32),
            pltpu.SemaphoreType.DMA((5 + PIECES,)),
        ),
        (leaf_t, node_t, right_side, basis, conductivity),
        written=1,
    )
    got = lax.all_to_all(sent, AXES, 0, 0)
    held = pltpu.VMEM((LBX, count_s * extent_x // LBX, extent_y), F32)
    near, down_high, down_low, meet_high, meet_low, inverse = call(
        window_kernel,
        (
            in_vmem(*field),
            *pair((levels + 1) * rank, rank),
            *pair(rank, (levels + 1) * rank),
            in_vmem(*leaf_inverse.shape),
        ),
        (right_side, up_high, up_low),
        10**7,
        (
            pltpu.VMEM((levels, rank, rank), F32),
            pltpu.VMEM((levels + 1, rank, rank), F32),
            held,
            pltpu.SemaphoreType.DMA((5,)),
        ),
        (leaf_f, node_f, leaf_inverse, leaf_t, node_t),
    )
    edge = (count_s + 1, extent_y)
    first_z, x_inner, x_outer, y_inner, y_outer, sums = call(
        first_kernel,
        [in_vmem(*s) for s in (field, edge, edge, (extent_x, extent_y), (extent_x, extent_y), (count_s, extent_y))],
        (got, own, down_high, down_low, wide_high, wide_low, near, right_side, conductivity),
        10**6,
    )
    pairs = matchings()
    x_inner, x_outer = swap(x_inner, pairs["gx_inner"]), swap(x_outer, pairs["gx_outer"])
    y_inner, y_outer = swap(y_inner, pairs["gy_inner"]), swap(y_outer, pairs["gy_outer"])
    applied, near, sent, home = call(
        second_kernel,
        (
            in_vmem(*field),
            in_vmem(*field),
            in_vmem(count, levels + 1, count_s, rank),
            in_vmem(count_s, rank),
        ),
        (
            x_inner, x_outer, y_inner, y_outer, first_z, conductivity,
            wide_high, wide_low, meet_high, meet_low, inverse, sums,
        ),
        10**6,
        (held,),
    )
    got = lax.all_to_all(sent, AXES, 0, 0)
    return call(
        last_kernel,
        (in_hbm(*field),) * 3,
        (got, home, meet_high, meet_low, wide_high, wide_low, near, first_z, right_side, applied),
        10**6,
        (pltpu.VMEM(field, F32),) * 4 + (pltpu.SemaphoreType.DMA((4,)),),
        written=3,
    )


def solution(mesh):
    return jax.shard_map(
        on_device,
        mesh=mesh,
        in_specs=(
            P(None, "gx", "gy"),
            P("gx", "gy"),
            P("gx", "gy", None, None),
            P("gx", "gy", None),
            P("gx", "gy", None, None),
            P("gx", "gy", None, None, None),
            P("gx", "gy", None, None),
            P("gx", "gy", None, None, None),
        ),
        out_specs=(P(None, "gx", "gy"), P(None, "gx", "gy"), P(None, "gx", "gy")),
        check_vma=False,
    )
```
